256 devices in a mesh: slab: 64 (over y, x_lo, z), view: 4 (over x_hi, core).
Axes of the slice: x: 4 (x_hi: 2, x_lo: 2; x = x_hi * 2 + x_lo), y: 4, z: 8, core: 2. Of those that a mesh axis runs over, the one named last changes fastest.
Arguments:
- primal: float32 [5, 256, 32, 128], P(None, 'slab', 'view'), may hold values from -6 to 6
- dual: bfloat16 [64, 256, 128], P('view', 'slab'), may hold values from -6 to 6
- footprints: bfloat16 [8, 128, 128], replicated, may hold values from -0.046875 to 0.046875
- tile_index: int32 [64, 8192, 2], P(None, 'slab'), may hold values from 0 to 3
- footprint_offset: int32 [64, 8192, 2], P(None, 'slab'), may hold values from 0 to 7
- w_first: bfloat16 [3, 3, 3, 32, 6], replicated, may hold values from -0.21875 to 0.21875
- w_middle: bfloat16 [3, 3, 3, 32, 32], replicated, may hold values from -0.21875 to 0.21875
- w_last: bfloat16 [3, 3, 3, 5, 32], replicated, may hold values from -0.5 to 0.5
- cotangent: float32 [5, 256, 32, 128], P(None, 'slab', 'view'), may hold values from -6 to 6
Outputs:
- d_primal: float32 [5, 256, 32, 128], P(None, 'slab', 'view')
- d_dual: float32 [64, 256, 128], P('view', 'slab')
- d_first: float32 [3, 3, 3, 32, 6], replicated
- d_middle: float32 [3, 3, 3, 32, 32], replicated
- d_last: float32 [3, 3, 3, 5, 32], replicated
The draws below stay inside these ranges and needn't reach their ends.
All inputs are finite; a program needn't handle non-finite values.
Results may differ from the reference program's by a relative error of at most 0.0067.
Values may be sent and summed in bfloat16 or wider, within the bound.
No kernel may reach another device: no remote copies, remote signals or barrier semaphores. Data moves between devices by JAX's collectives and lax.ppermute only.
A program may use at most 64 MiB of HBM per device.

```python
import jax
import jax.numpy as jnp
from jax import lax

PRIMAL = 5
HIDDEN_SIZE = 32
BIN = 128
NF = 8
TAPS = 2
DT = 4
CZ = 4
PX = 128
NZ = 256
NY = 32
VIEWS = 64
DTILES = 256
TILES = 8192


def set_ends(drawn, rng, least, largest):
    dims = drawn.shape
    place = [jax.random.randint(jax.random.fold_in(rng, axis), (), 0, dims[axis]) for axis in range(len(dims))]
    drawn = drawn.at[tuple(place)].set(least)
    longest = dims.index(max(dims))
    place[longest] = (place[longest] + 1) % dims[longest]
    return drawn.at[tuple(place)].set(largest)


def block_scale(rng, shape, shards, smallest, largest):
    loudness = 1.0
    for dim, shards_of in shards:
        steps = jax.random.uniform(jax.random.fold_in(jax.random.fold_in(rng, 6), dim), (shards_of,), jnp.float32, smallest / len(shards), largest / len(shards))
        loudness = loudness * jnp.repeat(jnp.exp(steps), shape[dim] // shards_of).reshape((-1,) + (1,) * (len(shape) - 1 - dim))
    return loudness


def gaussian(rng, shape, deviation, bound, pieces=(), kind=jnp.bfloat16):
    factor_of = block_scale(rng, shape, pieces, -0.22, 0.18) if pieces else 1.0
    drawn = jax.random.normal(rng, shape, jnp.float32) * deviation * factor_of
    return jnp.minimum(jnp.maximum(drawn, -bound), bound).astype(kind)


def setup_inputs(seed: int = 0) -> dict:
    streams_of = jax.random.split(jax.random.key(seed), 10)
    return {
        "primal": gaussian(streams_of[0], (PRIMAL, NZ, NY, PX), 1.0, 6.0, ((1, 64), (2, 4)), jnp.float32),
        "dual": gaussian(streams_of[1], (VIEWS, DTILES, BIN), 1.0, 6.0, ((0, 4), (1, 64))),
        "footprints": gaussian(streams_of[2], (NF, BIN, BIN), (BIN * VIEWS * TAPS) ** -0.5, 0.046875),
        "tile_index": set_ends(jax.random.randint(streams_of[3], (VIEWS, TILES, TAPS), 0, DT), jax.random.fold_in(streams_of[3], 1), 0, DT - 1).astype(jnp.int32),
        "footprint_offset": set_ends(jax.random.randint(streams_of[4], (VIEWS, TILES, TAPS), 0, NF), jax.random.fold_in(streams_of[4], 1), 0, NF - 1).astype(jnp.int32),
        "w_first": gaussian(streams_of[5], (3, 3, 3, HIDDEN_SIZE, PRIMAL + 1), (27 * HIDDEN_SIZE) ** -0.5, 0.21875),
        "w_middle": gaussian(streams_of[6], (3, 3, 3, HIDDEN_SIZE, HIDDEN_SIZE), (27 * HIDDEN_SIZE) ** -0.5, 0.21875),
        "w_last": gaussian(streams_of[7], (3, 3, 3, PRIMAL, HIDDEN_SIZE), (27 * PRIMAL) ** -0.5, 0.5),
        "cotangent": gaussian(streams_of[8], (PRIMAL, NZ, NY, PX), 1.0, 6.0, ((1, 64), (2, 4)), jnp.float32),
    }


def silu_slope(value):
    sig = jax.nn.sigmoid(value)
    return sig * (1.0 + value * (1.0 - sig))

def flipped(kernel):
    return kernel[::-1, ::-1, ::-1].transpose(0, 1, 2, 4, 3)

def pad_field(field):
    return jnp.pad(field, ((0, 0), (1, 1), (1, 1), (1, 1)))

def conv_ref(padded, kernel):
    kernel32 = kernel.astype(jnp.float32)

    def one_slice(zpos):
        window = lax.dynamic_slice_in_dim(padded, zpos, 3, 1).astype(jnp.float32)
        total = jnp.zeros((kernel.shape[3], NY, PX), jnp.float32)
        for za in range(3):
            for yb in range(3):
                for xc in range(3):
                    total = total + jnp.einsum('oc,cyx->oyx', kernel32[za, yb, xc], window[:, za, yb:yb + NY, xc:xc + PX], precision=lax.Precision.HIGHEST)
        return total
    slices = lax.map(one_slice, jnp.arange(NZ, dtype=jnp.int32))
    return slices.transpose(1, 0, 2, 3)

def grad_ref(dout, padded):

    def add_slice(total, zpos):
        window = lax.dynamic_slice_in_dim(padded, zpos, 3, 1).astype(jnp.float32)
        upper = lax.dynamic_index_in_dim(dout, zpos, 1, keepdims=False).astype(jnp.float32)
        terms = []
        for za in range(3):
            for yb in range(3):
                for xc in range(3):
                    terms.append(jnp.einsum('oyx,cyx->oc', upper, window[:, za, yb:yb + NY, xc:xc + PX], precision=lax.Precision.HIGHEST))
        return (total + jnp.stack(terms).reshape(3, 3, 3, dout.shape[0], padded.shape[0]), None)
    start = jnp.zeros((3, 3, 3, dout.shape[0], padded.shape[0]), jnp.float32)
    total, unused = lax.scan(add_slice, start, jnp.arange(NZ, dtype=jnp.int32))
    return total

def reference(primal, dual, footprints, tile_index, footprint_offset, w_first, w_middle, w_last, cotangent):
    x_tiles = PX // BIN
    forward_mat = footprints.transpose(1, 0, 2).reshape(BIN, NF * BIN)
    backward_mat = footprints.transpose(2, 0, 1).reshape(BIN, NF * BIN)
    heights = jnp.dot(dual.reshape(VIEWS * DTILES, BIN), forward_mat, preferred_element_type=jnp.float32).reshape(VIEWS * DTILES * NF, BIN)
    slab_of_tile = jnp.arange(TILES, dtype=jnp.int32) // (NY * x_tiles) // CZ

    def add_view(total, view):
        rows_idx = ((view * DTILES + slab_of_tile[:, None] * DT + tile_index[view]) * NF + footprint_offset[view]).astype(jnp.int32)
        return (total + jnp.take(heights, rows_idx, axis=0).sum(axis=1), None)
    back, unused = lax.scan(add_view, jnp.zeros((TILES, BIN), jnp.float32), jnp.arange(VIEWS, dtype=jnp.int32))
    back = back.reshape(NZ, NY, PX)
    x_zero = jnp.concatenate([primal, back[None]], axis=0).astype(jnp.bfloat16)
    x_pad = pad_field(x_zero)
    a_one = conv_ref(x_pad, w_first)
    z_one = jax.nn.silu(a_one).astype(jnp.bfloat16)
    z_one_pad = pad_field(z_one)
    a_two = conv_ref(z_one_pad, w_middle)
    z_two = jax.nn.silu(a_two).astype(jnp.bfloat16)
    g_low = cotangent.astype(jnp.bfloat16)
    dz_two = conv_ref(pad_field(g_low), flipped(w_last))
    d_last = grad_ref(g_low, pad_field(z_two))
    da_two = (dz_two * silu_slope(a_two)).astype(jnp.bfloat16)
    dz_one = conv_ref(pad_field(da_two), flipped(w_middle))
    d_middle = grad_ref(da_two, z_one_pad)
    da_one = (dz_one * silu_slope(a_one)).astype(jnp.bfloat16)
    dx_zero = conv_ref(pad_field(da_one), flipped(w_first))
    d_first = grad_ref(da_one, x_pad)
    d_primal = cotangent + dx_zero[:PRIMAL]
    strip_grad = dx_zero[PRIMAL].astype(jnp.bfloat16).reshape(TILES, BIN)
    proj = jnp.dot(strip_grad, backward_mat, preferred_element_type=jnp.float32).reshape(TILES * NF, BIN)
    tile_ids = jnp.arange(TILES, dtype=jnp.int32)

    def view_grad(view):
        source = (tile_ids[:, None] * NF + footprint_offset[view]).astype(jnp.int32)
        target = (slab_of_tile[:, None] * DT + tile_index[view]).astype(jnp.int32)
        return jax.ops.segment_sum(jnp.take(proj, source.reshape(-1), axis=0), target.reshape(-1), num_segments=DTILES)
    d_dual = lax.map(view_grad, jnp.arange(VIEWS, dtype=jnp.int32))
    scale = 1.0 / jnp.sqrt(jnp.float32(NZ * NY * PX))
    return (d_primal, d_dual, d_first * scale, d_middle * scale, d_last * scale)
```

```python
import math

import jax
import jax.numpy as jnp
from jax import lax
from jax.experimental import pallas as pl
from jax.experimental.pallas import tpu as pltpu
from jax.sharding import PartitionSpec as P

F32 = jnp.float32
BF16 = jnp.bfloat16
INTERPRET = False
PARAMS = pltpu.CompilerParams(vmem_limit_bytes=48 << 20)

CZ = 4
RY = 8
REACH = 4
WY = RY + 2 * REACH
LANES = 128
HID = 32
SLOT = 16
DTL = 4


def smem_spec():
    return pl.BlockSpec(memory_space=pltpu.SMEM)


def vmem_spec():
    return pl.BlockSpec(memory_space=pltpu.VMEM)


def gather_kernel(meta, packed, tiles, foots, prints, out, codes, duals, field, rows):
    view_at = meta[0]
    foot_count = prints.shape[0]
    views = tiles.shape[0] // 2
    codes[...] = (tiles[...] * foot_count + foots[...]).astype(F32)
    by_tap = jnp.concatenate(
        [codes[pl.ds(0, views, stride=2), :], codes[pl.ds(1, views, stride=2), :]], axis=0
    )
    by_tile = by_tap.T
    ranks = packed.shape[0]
    local = views // ranks * DTL
    for d in range(ranks):
        duals[d * local : (d + 1) * local, :] = packed[d, 320 : 320 + local, :].astype(F32)
    stack = []
    for g in range(DTL):
        one = duals[pl.ds(g, views, stride=DTL), :].astype(BF16)
        stack += [one, one]
    dual_rows = jnp.concatenate(stack, axis=0)
    back = jnp.zeros((by_tile.shape[0], LANES), F32)
    for o in range(foot_count):
        counts = jnp.concatenate(
            [
                jnp.where(by_tile == float(g * foot_count + o), 1.0, 0.0).astype(BF16)
                for g in range(DTL)
            ],
            axis=1,
        )
        part = jnp.dot(counts, dual_rows, preferred_element_type=F32)
        high = part.astype(BF16)
        low = (part - high.astype(F32)).astype(BF16)
        back = back + jnp.dot(high, prints[o], preferred_element_type=F32)
        back = back + jnp.dot(low, prints[o], preferred_element_type=F32)
    field[...] = back

    rows[...] = jnp.zeros(rows.shape, F32)
    before = jnp.maximum(view_at - 1, 0)
    after = jnp.minimum(view_at + 1, ranks - 1)
    has_before = view_at > 0
    has_after = view_at < ranks - 1
    full_y = RY * ranks

    def place(z, slot, mid, low_side, high_side):
        base = z * WY * SLOT + slot
        rows[pl.ds(base, REACH, stride=SLOT), :] = jnp.where(has_before, low_side[RY - REACH :], 0.0)
        rows[pl.ds(base + REACH * SLOT, RY, stride=SLOT), :] = mid
        rows[pl.ds(base + (REACH + RY) * SLOT, REACH, stride=SLOT), :] = jnp.where(
            has_after, high_side[:REACH], 0.0
        )

    for c in range(10):
        slot = c if c < 5 else c + 3
        mid = packed[view_at, c * 32 : c * 32 + 32, :].astype(F32)
        low_side = packed[before, c * 32 : c * 32 + 32, :].astype(F32)
        high_side = packed[after, c * 32 : c * 32 + 32, :].astype(F32)
        for z in range(CZ):
            cut = slice(z * RY, z * RY + RY)
            place(z, slot, mid[cut], low_side[cut], high_side[cut])
    for z in range(CZ):
        at = lambda rank: field[pl.ds(pl.multiple_of(z * full_y + rank * RY, RY), RY), :]
        place(z, 5, at(view_at), at(before), at(after))
    out[...] = rows[...].reshape(out.shape).astype(BF16)


def lane_masks(shape):
    lane = lax.broadcasted_iota(jnp.int32, shape, 1)
    return lane == 0, lane == LANES - 1


def shifted(value, first, last):
    left = jnp.where(first, 0.0, pltpu.roll(value, 1, 1))
    right = jnp.where(last, 0.0, pltpu.roll(value, LANES - 1, 1))
    return left, value, right


def shift_sum(taps, first, last):
    step = taps.shape[0] // 3
    left = jnp.where(first, 0.0, pltpu.roll(taps[:step], 1, 1))
    right = jnp.where(last, 0.0, pltpu.roll(taps[2 * step :], LANES - 1, 1))
    return taps[step : 2 * step] + left + right


def window(ref, width, z, y):
    sides = []
    for ahead in range(2):
        sides.append(
            jnp.concatenate(
                [ref[(z + a) * width + y + ahead + b] for a in range(3) for b in range(3)], axis=0
            )
        )
    return jnp.concatenate(sides, axis=1)


def net_kernel(
    meta, prev, here, following, cot, w_in, w_mid, w_mid_flip, w_first_flip,
    d_primal, strip, grads,
    box, slope, dz_two, z_one, z_two, da_two, da_one, dx,
):
    slab_at, view_at, slabs, ranks = meta[0], meta[1], meta[2], meta[3]
    per = CZ * WY
    box[0:per] = jnp.where(slab_at > 0, prev[...], jnp.zeros_like(prev[...]))
    box[per : 2 * per] = here[...]
    box[2 * per : 3 * per] = jnp.where(
        slab_at < slabs - 1, following[...], jnp.zeros_like(following[...])
    )
    first, last = lane_masks((HID, LANES))
    z_start, y_start = slab_at * CZ, view_at * RY
    z_end, y_end = slabs * CZ, ranks * RY

    def inside(z, y, reach):
        zz, yy = z_start - reach + z, y_start - reach + y
        return (zz >= 0) & (zz < z_end) & (yy >= 0) & (yy < y_end)

    def sigmoid(value):
        return 0.5 * jnp.tanh(0.5 * value) + 0.5

    depth3, rows3 = CZ + 6, RY + 6
    depth2, rows2 = CZ + 4, RY + 4
    depth1, rows1 = CZ + 2, RY + 2

    def layer_one(z, carry):
        for y in range(0, rows3, 2):
            taps = jnp.dot(w_in[...], window(box, WY, z, y), preferred_element_type=F32)
            for s in range(2):
                half = taps[:, s * LANES : (s + 1) * LANES]
                value = shift_sum(half[: 3 * HID], first, last)
                sig = sigmoid(value)
                at = z * rows3 + y + s
                z_one[at] = jnp.where(inside(z, y + s, 3), value * sig, 0.0).astype(BF16)
                slope[at] = sig * (1.0 + value * (1.0 - sig))
                dz_two[at] = shift_sum(half[3 * HID :], first, last)
        return carry

    lax.fori_loop(0, depth3, layer_one, 0)

    def layer_two(z, carry):
        for y in range(0, rows2, 2):
            taps = jnp.dot(w_mid[...], window(z_one, rows3, z, y), preferred_element_type=F32)
            for s in range(2):
                value = shift_sum(taps[:, s * LANES : (s + 1) * LANES], first, last)
                sig = sigmoid(value)
                at = z * rows2 + y + s
                z_two[at] = (value * sig).astype(BF16)
                grad = dz_two[(z + 1) * rows3 + y + s + 1] * (sig * (1.0 + value * (1.0 - sig)))
                da_two[at] = jnp.where(inside(z, y + s, 2), grad, 0.0).astype(BF16)
        return carry

    lax.fori_loop(0, depth2, layer_two, 0)

    def layer_back(z, carry):
        for y in range(0, rows1, 2):
            taps = jnp.dot(w_mid_flip[...], window(da_two, rows2, z, y), preferred_element_type=F32)
            for s in range(2):
                value = shift_sum(taps[:, s * LANES : (s + 1) * LANES], first, last)
                grad = value * slope[(z + 2) * rows3 + y + s + 2]
                da_one[z * rows1 + y + s] = jnp.where(inside(z, y + s, 1), grad, 0.0).astype(BF16)
        return carry

    lax.fori_loop(0, depth1, layer_back, 0)

    first8, last8 = lane_masks((8, LANES))
    grads[...] = jnp.zeros(grads.shape, F32)

    def layer_out(z, carry):
        for y in range(0, RY, 2):
            taps = jnp.dot(w_first_flip[...], window(da_one, rows1, z, y), preferred_element_type=F32)
            for s in range(2):
                at = pl.multiple_of((z * RY + y + s) * 8, 8)
                dx[pl.ds(at, 8), :] = shift_sum(taps[:, s * LANES : (s + 1) * LANES], first8, last8)
        blank = jnp.zeros((HID, LANES), BF16)
        ends, mids, low, mid = [], [], [], []
        for y in range(0, RY, 2):
            low.append(window(box, WY, z + 3, y + 3))
            mid.append(window(da_two, rows2, z + 1, y + 1))
            for s in range(2):
                one = da_one[(z + 1) * rows1 + y + s + 1].astype(F32)
                two = z_two[(z + 2) * rows2 + y + s + 2].astype(F32)
                inner = z_one[(z + 3) * rows3 + y + s + 3].astype(F32)
                back = lambda v: [p.astype(BF16) for p in shifted(v, first, last)[::-1]]
                ends.append(jnp.concatenate(back(one) + [blank] + back(two) + [blank], axis=0))
                mids.append(jnp.concatenate(back(inner) + [blank], axis=0))
        contract = (((1,), (1,)), ((), ()))
        out = lax.dot_general(
            jnp.concatenate(low, axis=1), jnp.concatenate(ends, axis=1), contract,
            preferred_element_type=F32,
        )
        for tap in range(9):
            x_rows = slice(tap * SLOT, tap * SLOT + 8)
            g_rows = slice(tap * SLOT + 8, tap * SLOT + 16)
            grads[288 + tap * SLOT : 288 + tap * SLOT + 8, :] += out[x_rows, :LANES]
            grads[288 + tap * SLOT + 8 : 288 + tap * SLOT + 16, :] += out[g_rows, LANES:]
        grads[0:288, :] += lax.dot_general(
            jnp.concatenate(mid, axis=1), jnp.concatenate(mids, axis=1), contract,
            preferred_element_type=F32,
        )
        return carry

    lax.fori_loop(0, CZ, layer_out, 0)

    for z in range(CZ):
        for c in range(5):
            d_primal[c, z] = cot[c, z] + dx[pl.ds(z * RY * 8 + c, RY, stride=8), :]
        strip[z * RY : (z + 1) * RY, :] = dx[pl.ds(z * RY * 8 + 5, RY, stride=8), :]


def dual_kernel(meta, strips, tiles, foots, prints, out, codes):
    view_at = meta[0]
    foot_count = prints.shape[0]
    ranks = strips.shape[0]
    views = tiles.shape[0] // 2 // ranks
    own = pl.ds(pl.multiple_of(view_at * views * 2, views * 2), views * 2)
    codes[...] = (tiles[own, :] * foot_count + foots[own, :]).astype(F32)
    taps = [codes[pl.ds(k, views, stride=2), :] for k in range(2)]
    pieces = [strips[d].astype(F32) for d in range(ranks)]
    field = jnp.concatenate(
        [pieces[d][z * RY : (z + 1) * RY] for z in range(CZ) for d in range(ranks)], axis=0
    ).astype(BF16)
    total = jnp.zeros((DTL * views, LANES), F32)
    contract = (((1,), (1,)), ((), ()))
    for o in range(foot_count):
        counts = jnp.concatenate(
            [
                sum(jnp.where(tap == float(g * foot_count + o), 1.0, 0.0) for tap in taps)
                for g in range(DTL)
            ],
            axis=0,
        ).astype(BF16)
        part = jnp.dot(counts, field, preferred_element_type=F32)
        high = part.astype(BF16)
        low = (part - high.astype(F32)).astype(BF16)
        both = lax.dot_general(
            jnp.concatenate([high, low], axis=0), prints[o], contract, preferred_element_type=F32
        )
        total = total + both[: DTL * views] + both[DTL * views :]
    for g in range(DTL):
        out[pl.ds(g, views, stride=DTL), :] = total[g * views : (g + 1) * views]


def split_kernel(scale, packed, d_first, d_middle, d_last):
    values = packed[0:432, :] * scale
    for shift in range(3):
        moved = values if shift == 0 else pltpu.roll(values, LANES - shift * HID, 1)
        for a in range(3):
            for b in range(3):
                tap = a * 3 + b
                d_middle[2 - a, 2 - b, 2 - shift] = moved[tap * HID : (tap + 1) * HID, :HID]
                at = 288 + tap * SLOT
                d_first[a, b, shift] = moved[at : at + 6, :HID]
                d_last[2 - a, 2 - b, 2 - shift] = moved[at + 8 : at + 13, :HID]


def split_call(scale):
    def kernel(*refs):
        split_kernel(scale, *refs)

    return kernel


def flipped(kernel):
    return kernel[::-1, ::-1, ::-1].transpose(0, 1, 2, 4, 3)


def by_rows(kernel, inputs_to, outputs_to, shift=0):
    o, i = kernel.shape[3], kernel.shape[4]
    kernel = jnp.pad(
        kernel, ((0, 0), (0, 0), (0, 0), (0, outputs_to - o), (shift, inputs_to - i - shift))
    )
    return kernel.transpose(2, 3, 0, 1, 4).reshape(3 * outputs_to, 9 * inputs_to)


def shards(
    primal, dual, footprints, tile_index, footprint_offset, w_first, w_middle, w_last, cotangent
):
    views_here, det_tiles, bins = dual.shape
    all_views, tiles_here, taps = tile_index.shape
    ranks = lax.axis_size("view")
    slabs = lax.axis_size("slab")
    devices = ranks * slabs
    view_at = lax.axis_index("view")
    slab_at = lax.axis_index("slab")
    meta = jnp.stack([view_at]).astype(jnp.int32)
    meta_net = jnp.stack([slab_at, view_at, slabs, ranks]).astype(jnp.int32)
    flat = lambda idx: idx.transpose(0, 2, 1).reshape(all_views * taps, tiles_here)
    tiles, foots = flat(tile_index), flat(footprint_offset)

    packed = jnp.concatenate(
        [
            primal.astype(BF16).reshape(160, LANES),
            cotangent.astype(BF16).reshape(160, LANES),
            dual.reshape(views_here * det_tiles, LANES),
        ],
        axis=0,
    )
    packed = lax.all_gather(packed, "view", axis=0, tiled=False)

    here = pl.pallas_call(
        gather_kernel,
        out_shape=jax.ShapeDtypeStruct((CZ * WY, SLOT, LANES), BF16),
        in_specs=[smem_spec()] + [vmem_spec()] * 4,
        out_specs=vmem_spec(),
        scratch_shapes=[
            pltpu.VMEM((all_views * taps, tiles_here), F32),
            pltpu.VMEM((all_views * det_tiles, LANES), F32),
            pltpu.VMEM((tiles_here, LANES), F32),
            pltpu.VMEM((CZ * WY * SLOT, LANES), F32),
        ],
        compiler_params=PARAMS,
        interpret=INTERPRET,
        name="box_rows",
    )(meta, packed, tiles, foots, footprints)

    prev = lax.ppermute(here, "slab", [(i, (i + 1) % slabs) for i in range(slabs)])
    following = lax.ppermute(here, "slab", [((i + 1) % slabs, i) for i in range(slabs)])

    w_in = jnp.concatenate(
        [by_rows(w_first, SLOT, HID), by_rows(flipped(w_last), SLOT, HID, 8)], axis=0
    )
    w_mid = by_rows(w_middle, HID, HID)
    w_mid_flip = by_rows(flipped(w_middle), HID, HID)
    w_first_flip = by_rows(flipped(w_first), HID, 8)

    rows3, rows2, rows1 = 140, 96, 60
    d_primal, strip, grads = pl.pallas_call(
        net_kernel,
        out_shape=(
            jax.ShapeDtypeStruct(primal.shape, F32),
            jax.ShapeDtypeStruct((CZ * RY, LANES), F32),
            jax.ShapeDtypeStruct((2 * devices if devices >= 216 else 32 * devices, LANES), F32),
        ),
        in_specs=[smem_spec()] + [vmem_spec()] * 8,
        out_specs=(vmem_spec(),) * 3,
        scratch_shapes=[
            pltpu.VMEM((3 * CZ * WY, SLOT, LANES), BF16),
            pltpu.VMEM((rows3, HID, LANES), F32),
            pltpu.VMEM((rows3, HID, LANES), F32),
            pltpu.VMEM((rows3, HID, LANES), BF16),
            pltpu.VMEM((rows2, HID, LANES), BF16),
            pltpu.VMEM((rows2, HID, LANES), BF16),
            pltpu.VMEM((rows1, HID, LANES), BF16),
            pltpu.VMEM((CZ * RY * 8, LANES), F32),
        ],
        compiler_params=PARAMS,
        interpret=INTERPRET,
        name="net_box",
    )(meta_net, prev, here, following, cotangent, w_in, w_mid, w_mid_flip, w_first_flip)

    strip = strip.astype(BF16)
    ring = lambda step: [(i, (i + step) % ranks) for i in range(ranks)]
    others = [lax.ppermute(strip, "view", ring(step)) for step in range(1, ranks)]

    both = ("slab", "view")
    per = grads.shape[0] // devices
    shares = lax.all_to_all(grads.reshape(devices, per, LANES), both, 0, 0, tiled=True)
    summed = shares.sum(axis=0)
    whole = lax.all_to_all(
        jnp.broadcast_to(summed[None], shares.shape), both, 0, 0, tiled=True
    ).reshape(grads.shape)

    arrived = jnp.stack([strip] + others)
    order = (view_at - jnp.arange(ranks)) % ranks
    strips = jnp.take(arrived, order, axis=0)
    d_dual = pl.pallas_call(
        dual_kernel,
        out_shape=jax.ShapeDtypeStruct((views_here * det_tiles, LANES), F32),
        in_specs=[smem_spec()] + [vmem_spec()] * 4,
        out_specs=vmem_spec(),
        scratch_shapes=[pltpu.VMEM((views_here * taps, tiles_here), F32)],
        compiler_params=PARAMS,
        interpret=INTERPRET,
        name="dual_views",
    )(meta, strips, tiles, foots, footprints)

    full = slabs * CZ * ranks * RY * LANES
    d_first, d_middle, d_last = pl.pallas_call(
        split_call(1.0 / math.sqrt(full)),
        out_shape=(
            jax.ShapeDtypeStruct((3, 3, 3, 6, HID), F32),
            jax.ShapeDtypeStruct((3, 3, 3, HID, HID), F32),
            jax.ShapeDtypeStruct((3, 3, 3, 5, HID), F32),
        ),
        in_specs=[vmem_spec()],
        out_specs=(vmem_spec(),) * 3,
        compiler_params=PARAMS,
        interpret=INTERPRET,
        name="split_grads",
    )(whole)
    return (
        d_primal,
        d_dual.reshape(dual.shape),
        d_first.transpose(0, 1, 2, 4, 3),
        d_middle,
        d_last,
    )


def solution(mesh):
    placed = (
        P(None, "slab", "view", None),
        P("view", "slab", None),
        P(),
        P(None, "slab", None),
        P(None, "slab", None),
        P(),
        P(),
        P(),
        P(None, "slab", "view", None),
    )
    return jax.shard_map(
        shards,
        mesh=mesh,
        in_specs=placed,
        out_specs=(P(None, "slab", "view", None), P("view", "slab", None), P(), P(), P()),
        check_vma=False,
    )
```

```python
import math

import jax
import jax.numpy as jnp
from jax import lax
from jax.experimental import pallas as pl
from jax.experimental.pallas import tpu as pltpu
from jax.sharding import PartitionSpec as P

F32 = jnp.float32
BF16 = jnp.bfloat16
INTERPRET = False
PARAMS = pltpu.CompilerParams(vmem_limit_bytes=48 << 20)

CZ = 4
RY = 8
REACH = 4
WY = RY + 2 * REACH
LANES = 128
HID = 32
SLOT = 16
DTL = 4


def smem_spec():
    return pl.BlockSpec(memory_space=pltpu.SMEM)


def vmem_spec():
    return pl.BlockSpec(memory_space=pltpu.VMEM)


def gather_kernel(meta, packed, tiles, foots, prints, out, codes, duals, field, rows):
    view_at = meta[0]
    foot_count = prints.shape[0]
    views = tiles.shape[0] // 2
    codes[...] = (tiles[...] * foot_count + foots[...]).astype(F32)
    by_tap = jnp.concatenate(
        [codes[pl.ds(0, views, stride=2), :], codes[pl.ds(1, views, stride=2), :]], axis=0
    )
    by_tile = by_tap.T
    ranks = packed.shape[0]
    local = views // ranks * DTL
    for d in range(ranks):
        duals[d * local : (d + 1) * local, :] = packed[d, 320 : 320 + local, :].astype(F32)
    stack = []
    for g in range(DTL):
        one = duals[pl.ds(g, views, stride=DTL), :].astype(BF16)
        stack += [one, one]
    dual_rows = jnp.concatenate(stack, axis=0)
    back = jnp.zeros((by_tile.shape[0], LANES), F32)
    for o in range(foot_count):
        counts = jnp.concatenate(
            [
                jnp.where(by_tile == float(g * foot_count + o), 1.0, 0.0).astype(BF16)
                for g in range(DTL)
            ],
            axis=1,
        )
        part = jnp.dot(counts, dual_rows, preferred_element_type=F32)
        high = part.astype(BF16)
        low = (part - high.astype(F32)).astype(BF16)
        back = back + jnp.dot(high, prints[o], preferred_element_type=F32)
        back = back + jnp.dot(low, prints[o], preferred_element_type=F32)
    field[...] = back

    rows[...] = jnp.zeros(rows.shape, F32)
    before = jnp.maximum(view_at - 1, 0)
    after = jnp.minimum(view_at + 1, ranks - 1)
    has_before = view_at > 0
    has_after = view_at < ranks - 1
    full_y = RY * ranks

    def place(z, slot, mid, low_side, high_side):
        base = z * WY * SLOT + slot
        rows[pl.ds(base, REACH, stride=SLOT), :] = jnp.where(has_before, low_side[RY - REACH :], 0.0)
        rows[pl.ds(base + REACH * SLOT, RY, stride=SLOT), :] = mid
        rows[pl.ds(base + (REACH + RY) * SLOT, REACH, stride=SLOT), :] = jnp.where(
            has_after, high_side[:REACH], 0.0
        )

    for c in range(10):
        slot = c if c < 5 else c + 3
        mid = packed[view_at, c * 32 : c * 32 + 32, :].astype(F32)
        low_side = packed[before, c * 32 : c * 32 + 32, :].astype(F32)
        high_side = packed[after, c * 32 : c * 32 + 32, :].astype(F32)
        for z in range(CZ):
            cut = slice(z * RY, z * RY + RY)
            place(z, slot, mid[cut], low_side[cut], high_side[cut])
    for z in range(CZ):
        at = lambda rank: field[pl.ds(pl.multiple_of(z * full_y + rank * RY, RY), RY), :]
        place(z, 5, at(view_at), at(before), at(after))
    out[...] = rows[...].reshape(out.shape).astype(BF16)


def lane_masks(shape):
    lane = lax.broadcasted_iota(jnp.int32, shape, 1)
    return lane == 0, lane == LANES - 1


def shifted(value, first, last):
    left = jnp.where(first, 0.0, pltpu.roll(value, 1, 1))
    right = jnp.where(last, 0.0, pltpu.roll(value, LANES - 1, 1))
    return left, value, right


def shift_sum(taps, first, last):
    step = taps.shape[0] // 3
    left = jnp.where(first, 0.0, pltpu.roll(taps[:step], 1, 1))
    right = jnp.where(last, 0.0, pltpu.roll(taps[2 * step :], LANES - 1, 1))
    return taps[step : 2 * step] + left + right


def window(ref, width, z, y):
    sides = []
    for ahead in range(2):
        sides.append(
            jnp.concatenate(
                [ref[(z + a) * width + y + ahead + b] for a in range(3) for b in range(3)], axis=0
            )
        )
    return jnp.concatenate(sides, axis=1)


def net_kernel(
    meta, prev, here, following, cot, w_in, w_mid, w_mid_flip, w_first_flip,
    d_primal, strip, packed,
    grads, box, slope, dz_two, z_one, z_two, da_two, da_one, dx,
):
    slab_at, view_at, slabs, ranks = meta[0], meta[1], meta[2], meta[3]
    per = CZ * WY
    box[0:per] = prev[...]
    box[per : 2 * per] = here[...]
    box[2 * per : 3 * per] = following[...]
    first, last = lane_masks((HID, LANES))
    z_start, y_start = slab_at * CZ, view_at * RY
    z_end, y_end = slabs * CZ, ranks * RY

    def inside(z, y, reach):
        zz, yy = z_start - reach + z, y_start - reach + y
        return (zz >= 0) & (zz < z_end) & (yy >= 0) & (yy < y_end)

    def sigmoid(value):
        return 0.5 * jnp.tanh(0.5 * value) + 0.5

    depth3, rows3 = CZ + 6, RY + 6
    depth2, rows2 = CZ + 4, RY + 4
    depth1, rows1 = CZ + 2, RY + 2

    def layer_one(z, carry):
        for y in range(0, rows3, 2):
            taps = jnp.dot(w_in[...], window(box, WY, z, y), preferred_element_type=F32)
            for s in range(2):
                half = taps[:, s * LANES : (s + 1) * LANES]
                value = shift_sum(half[: 3 * HID], first, last)
                sig = sigmoid(value)
                at = z * rows3 + y + s
                z_one[at] = jnp.where(inside(z, y + s, 3), value * sig, 0.0).astype(BF16)
                slope[at] = sig * (1.0 + value * (1.0 - sig))
                dz_two[at] = shift_sum(half[3 * HID :], first, last)
        return carry

    lax.fori_loop(0, depth3, layer_one, 0)

    def layer_two(z, carry):
        for y in range(0, rows2, 2):
            taps = jnp.dot(w_mid[...], window(z_one, rows3, z, y), preferred_element_type=F32)
            for s in range(2):
                value = shift_sum(taps[:, s * LANES : (s + 1) * LANES], first, last)
                sig = sigmoid(value)
                at = z * rows2 + y + s
                z_two[at] = (value * sig).astype(BF16)
                grad = dz_two[(z + 1) * rows3 + y + s + 1] * (sig * (1.0 + value * (1.0 - sig)))
                da_two[at] = jnp.where(inside(z, y + s, 2), grad, 0.0).astype(BF16)
        return carry

    lax.fori_loop(0, depth2, layer_two, 0)

    def layer_back(z, carry):
        for y in range(0, rows1, 2):
            taps = jnp.dot(w_mid_flip[...], window(da_two, rows2, z, y), preferred_element_type=F32)
            for s in range(2):
                value = shift_sum(taps[:, s * LANES : (s + 1) * LANES], first, last)
                grad = value * slope[(z + 2) * rows3 + y + s + 2]
                da_one[z * rows1 + y + s] = jnp.where(inside(z, y + s, 1), grad, 0.0).astype(BF16)
        return carry

    lax.fori_loop(0, depth1, layer_back, 0)

    first8, last8 = lane_masks((8, LANES))
    grads[...] = jnp.zeros(grads.shape, F32)

    def layer_out(z, carry):
        for y in range(0, RY, 2):
            taps = jnp.dot(w_first_flip[...], window(da_one, rows1, z, y), preferred_element_type=F32)
            for s in range(2):
                at = pl.multiple_of((z * RY + y + s) * 8, 8)
                dx[pl.ds(at, 8), :] = shift_sum(taps[:, s * LANES : (s + 1) * LANES], first8, last8)
        blank = jnp.zeros((HID, LANES), BF16)
        ends, mids, low, mid = [], [], [], []
        for y in range(0, RY, 2):
            low.append(window(box, WY, z + 3, y + 3))
            mid.append(window(da_two, rows2, z + 1, y + 1))
            for s in range(2):
                one = da_one[(z + 1) * rows1 + y + s + 1].astype(F32)
                two = z_two[(z + 2) * rows2 + y + s + 2].astype(F32)
                inner = z_one[(z + 3) * rows3 + y + s + 3].astype(F32)
                back = lambda v: [p.astype(BF16) for p in shifted(v, first, last)[::-1]]
                ends.append(jnp.concatenate(back(one) + [blank] + back(two) + [blank], axis=0))
                mids.append(jnp.concatenate(back(inner) + [blank], axis=0))
        contract = (((1,), (1,)), ((), ()))
        out = lax.dot_general(
            jnp.concatenate(low, axis=1), jnp.concatenate(ends, axis=1), contract,
            preferred_element_type=F32,
        )
        for tap in range(9):
            x_rows = slice(tap * SLOT, tap * SLOT + 8)
            g_rows = slice(tap * SLOT + 8, tap * SLOT + 16)
            grads[288 + tap * SLOT : 288 + tap * SLOT + 8, :] += out[x_rows, :LANES]
            grads[288 + tap * SLOT + 8 : 288 + tap * SLOT + 16, :] += out[g_rows, LANES:]
        grads[0:288, :] += lax.dot_general(
            jnp.concatenate(mid, axis=1), jnp.concatenate(mids, axis=1), contract,
            preferred_element_type=F32,
        )
        return carry

    lax.fori_loop(0, CZ, layer_out, 0)

    for z in range(CZ):
        for c in range(5):
            d_primal[c, z] = cot[c, z] + dx[pl.ds(z * RY * 8 + c, RY, stride=8), :]
        strip[z * RY : (z + 1) * RY, :] = dx[pl.ds(z * RY * 8 + 5, RY, stride=8), :]
    packed[0 : grads.shape[0], :] = grads[...].astype(BF16)
    packed[grads.shape[0] :, :] = jnp.zeros((packed.shape[0] - grads.shape[0], LANES), BF16)


def dual_kernel(meta, strips, tiles, foots, prints, out, codes):
    view_at = meta[0]
    foot_count = prints.shape[0]
    ranks = strips.shape[0]
    views = tiles.shape[0] // 2 // ranks
    own = pl.ds(pl.multiple_of(view_at * views * 2, views * 2), views * 2)
    codes[...] = (tiles[own, :] * foot_count + foots[own, :]).astype(F32)
    taps = [codes[pl.ds(k, views, stride=2), :] for k in range(2)]
    pieces = [strips[d].astype(F32) for d in range(ranks)]
    field = jnp.concatenate(
        [pieces[d][z * RY : (z + 1) * RY] for z in range(CZ) for d in range(ranks)], axis=0
    ).astype(BF16)
    total = jnp.zeros((DTL * views, LANES), F32)
    contract = (((1,), (1,)), ((), ()))
    for o in range(foot_count):
        counts = jnp.concatenate(
            [
                sum(jnp.where(tap == float(g * foot_count + o), 1.0, 0.0) for tap in taps)
                for g in range(DTL)
            ],
            axis=0,
        ).astype(BF16)
        part = jnp.dot(counts, field, preferred_element_type=F32)
        high = part.astype(BF16)
        low = (part - high.astype(F32)).astype(BF16)
        both = lax.dot_general(
            jnp.concatenate([high, low], axis=0), prints[o], contract, preferred_element_type=F32
        )
        total = total + both[: DTL * views] + both[DTL * views :]
    for g in range(DTL):
        out[pl.ds(g, views, stride=DTL), :] = total[g * views : (g + 1) * views]


def sum_kernel(per, shares, out):
    block = max(per, 8)
    total = shares[...].astype(F32).reshape(shares.shape[0] // block, block, LANES).sum(axis=0)
    step = per
    while step < block:
        total = total + pltpu.roll(total, step, 0)
        step *= 2
    while total.shape[0] < 16:
        total = jnp.concatenate([total, total], axis=0)
    total = total.astype(BF16)
    for at in range(0, out.shape[0], total.shape[0]):
        out[at : at + total.shape[0], :] = total


def sum_call(per):
    def kernel(*refs):
        sum_kernel(per, *refs)

    return kernel


def split_kernel(scale, packed, d_first, d_middle, d_last):
    values = packed[0:432, :].astype(F32) * scale
    for shift in range(3):
        moved = values if shift == 0 else pltpu.roll(values, LANES - shift * HID, 1)
        for a in range(3):
            for b in range(3):
                tap = a * 3 + b
                d_middle[2 - a, 2 - b, 2 - shift] = moved[tap * HID : (tap + 1) * HID, :HID]
                at = 288 + tap * SLOT
                d_first[a, b, shift] = moved[at : at + 6, :HID]
                d_last[2 - a, 2 - b, :, 2 - shift, :] = moved[at + 8 : at + 13, :HID]


def split_call(scale):
    def kernel(*refs):
        split_kernel(scale, *refs)

    return kernel


def flipped(kernel):
    return kernel[::-1, ::-1, ::-1].transpose(0, 1, 2, 4, 3)


def by_rows(kernel, inputs_to, outputs_to, shift=0):
    o, i = kernel.shape[3], kernel.shape[4]
    kernel = jnp.pad(
        kernel, ((0, 0), (0, 0), (0, 0), (0, outputs_to - o), (shift, inputs_to - i - shift))
    )
    return kernel.transpose(2, 3, 0, 1, 4).reshape(3 * outputs_to, 9 * inputs_to)


def shards(
    primal, dual, footprints, tile_index, footprint_offset, w_first, w_middle, w_last, cotangent
):
    views_here, det_tiles, bins = dual.shape
    all_views, tiles_here, taps = tile_index.shape
    ranks = lax.axis_size("view")
    slabs = lax.axis_size("slab")
    devices = ranks * slabs
    view_at = lax.axis_index("view")
    slab_at = lax.axis_index("slab")
    meta = jnp.stack([view_at]).astype(jnp.int32)
    meta_net = jnp.stack([slab_at, view_at, slabs, ranks]).astype(jnp.int32)
    flat = lambda idx: idx.transpose(0, 2, 1).reshape(all_views * taps, tiles_here)
    tiles, foots = flat(tile_index), flat(footprint_offset)

    packed = jnp.concatenate(
        [
            primal.astype(BF16).reshape(160, LANES),
            cotangent.astype(BF16).reshape(160, LANES),
            dual.reshape(views_here * det_tiles, LANES),
        ],
        axis=0,
    )
    packed = lax.all_gather(packed, "view", axis=0, tiled=False)

    here = pl.pallas_call(
        gather_kernel,
        out_shape=jax.ShapeDtypeStruct((CZ * WY, SLOT, LANES), BF16),
        in_specs=[smem_spec()] + [vmem_spec()] * 4,
        out_specs=vmem_spec(),
        scratch_shapes=[
            pltpu.VMEM((all_views * taps, tiles_here), F32),
            pltpu.VMEM((all_views * det_tiles, LANES), F32),
            pltpu.VMEM((tiles_here, LANES), F32),
            pltpu.VMEM((CZ * WY * SLOT, LANES), F32),
        ],
        compiler_params=PARAMS,
        interpret=INTERPRET,
        name="box_rows",
    )(meta, packed, tiles, foots, footprints)

    prev = lax.ppermute(here, "slab", [(i, i + 1) for i in range(slabs - 1)])
    following = lax.ppermute(here, "slab", [(i + 1, i) for i in range(slabs - 1)])

    w_in = jnp.concatenate(
        [by_rows(w_first, SLOT, HID), by_rows(flipped(w_last), SLOT, HID, 8)], axis=0
    )
    w_mid = by_rows(w_middle, HID, HID)
    w_mid_flip = by_rows(flipped(w_middle), HID, HID)
    w_first_flip = by_rows(flipped(w_first), HID, 8)

    rows3, rows2, rows1 = 140, 96, 60
    d_primal, strip, grads = pl.pallas_call(
        net_kernel,
        out_shape=(
            jax.ShapeDtypeStruct(primal.shape, F32),
            jax.ShapeDtypeStruct((CZ * RY, LANES), F32),
            jax.ShapeDtypeStruct((2 * devices if devices >= 256 else 32 * devices, LANES), BF16),
        ),
        in_specs=[smem_spec()] + [vmem_spec()] * 8,
        out_specs=(vmem_spec(),) * 3,
        scratch_shapes=[
            pltpu.VMEM((432, LANES), F32),
            pltpu.VMEM((3 * CZ * WY, SLOT, LANES), BF16),
            pltpu.VMEM((rows3, HID, LANES), F32),
            pltpu.VMEM((rows3, HID, LANES), F32),
            pltpu.VMEM((rows3, HID, LANES), BF16),
            pltpu.VMEM((rows2, HID, LANES), BF16),
            pltpu.VMEM((rows2, HID, LANES), BF16),
            pltpu.VMEM((rows1, HID, LANES), BF16),
            pltpu.VMEM((CZ * RY * 8, LANES), F32),
        ],
        compiler_params=PARAMS,
        interpret=INTERPRET,
        name="net_box",
    )(meta_net, prev, here, following, cotangent, w_in, w_mid, w_mid_flip, w_first_flip)

    strip = strip.astype(BF16)
    ring = lambda step: [(i, (i + step) % ranks) for i in range(ranks)]
    others = [lax.ppermute(strip, "view", ring(step)) for step in range(1, ranks)]

    both = ("slab", "view")
    per = grads.shape[0] // devices
    shares = lax.all_to_all(grads.reshape(devices, per, LANES), both, 0, 0, tiled=True)
    summed = pl.pallas_call(
        sum_call(per),
        out_shape=jax.ShapeDtypeStruct(grads.shape, BF16),
        in_specs=[vmem_spec()],
        out_specs=vmem_spec(),
        compiler_params=PARAMS,
        interpret=INTERPRET,
        name="sum_shares",
    )(shares.reshape(grads.shape))
    whole = lax.all_to_all(
        summed.reshape(shares.shape), both, 0, 0, tiled=True
    ).reshape(grads.shape)

    arrived = jnp.stack([strip] + others)
    order = (view_at - jnp.arange(ranks)) % ranks
    strips = jnp.take(arrived, order, axis=0)
    d_dual = pl.pallas_call(
        dual_kernel,
        out_shape=jax.ShapeDtypeStruct((views_here * det_tiles, LANES), F32),
        in_specs=[smem_spec()] + [vmem_spec()] * 4,
        out_specs=vmem_spec(),
        scratch_shapes=[pltpu.VMEM((views_here * taps, tiles_here), F32)],
        compiler_params=PARAMS,
        interpret=INTERPRET,
        name="dual_views",
    )(meta, strips, tiles, foots, footprints)

    full = slabs * CZ * ranks * RY * LANES
    d_first, d_middle, d_last = pl.pallas_call(
        split_call(1.0 / math.sqrt(full)),
        out_shape=(
            jax.ShapeDtypeStruct((3, 3, 3, 6, HID), F32),
            jax.ShapeDtypeStruct((3, 3, 3, HID, HID), F32),
            jax.ShapeDtypeStruct((3, 3, 5, 3, HID), F32),
        ),
        in_specs=[vmem_spec()],
        out_specs=(vmem_spec(),) * 3,
        compiler_params=PARAMS,
        interpret=INTERPRET,
        name="split_grads",
    )(whole)
    return (
        d_primal,
        d_dual.reshape(dual.shape),
        d_first.transpose(0, 1, 2, 4, 3),
        d_middle,
        d_last.transpose(0, 1, 3, 2, 4),
    )


def solution(mesh):
    placed = (
        P(None, "slab", "view", None),
        P("view", "slab", None),
        P(),
        P(None, "slab", None),
        P(None, "slab", None),
        P(),
        P(),
        P(),
        P(None, "slab", "view", None),
    )
    return jax.shard_map(
        shards,
        mesh=mesh,
        in_specs=placed,
        out_specs=(P(None, "slab", "view", None), P("view", "slab", None), P(), P(), P()),
        check_vma=False,
    )
```

```python
import math

import jax
import jax.numpy as jnp
from jax import lax
from jax.experimental import pallas as pl
from jax.experimental.pallas import tpu as pltpu
from jax.sharding import PartitionSpec as P

F32 = jnp.float32
BF16 = jnp.bfloat16
INTERPRET = False
PARAMS = pltpu.CompilerParams(vmem_limit_bytes=48 << 20)

CZ = 4
RY = 8
REACH = 4
WY = RY + 2 * REACH
LANES = 128
HID = 32
SLOT = 16
DTL = 4


def smem_spec():
    return pl.BlockSpec(memory_space=pltpu.SMEM)


def vmem_spec():
    return pl.BlockSpec(memory_space=pltpu.VMEM)


def pack_kernel(primal, cotangent, dual, out):
    out[0:160, :] = primal[...].astype(BF16)
    out[160:320, :] = cotangent[...].astype(BF16)
    out[320:, :] = dual[...]


def gather_kernel(meta, packed, tiles, foots, prints, out, codes, duals, field, rows):
    view_at = meta[0]
    foot_count = prints.shape[0]
    views = tiles.shape[0] // 2
    codes[...] = (tiles[...] * foot_count + foots[...]).astype(F32)
    by_tap = jnp.concatenate(
        [codes[pl.ds(0, views, stride=2), :], codes[pl.ds(1, views, stride=2), :]], axis=0
    )
    by_tile = by_tap.T
    ranks = packed.shape[0]
    local = views // ranks * DTL
    for d in range(ranks):
        duals[d * local : (d + 1) * local, :] = packed[d, 320 : 320 + local, :].astype(F32)
    stack = []
    for g in range(DTL):
        one = duals[pl.ds(g, views, stride=DTL), :].astype(BF16)
        stack += [one, one]
    dual_rows = jnp.concatenate(stack, axis=0)
    back = jnp.zeros((by_tile.shape[0], LANES), F32)
    for o in range(foot_count):
        counts = jnp.concatenate(
            [
                jnp.where(by_tile == float(g * foot_count + o), 1.0, 0.0).astype(BF16)
                for g in range(DTL)
            ],
            axis=1,
        )
        part = jnp.dot(counts, dual_rows, preferred_element_type=F32)
        high = part.astype(BF16)
        low = (part - high.astype(F32)).astype(BF16)
        back = back + jnp.dot(high, prints[o], preferred_element_type=F32)
        back = back + jnp.dot(low, prints[o], preferred_element_type=F32)
    field[...] = back

    rows[...] = jnp.zeros(rows.shape, F32)
    before = jnp.maximum(view_at - 1, 0)
    after = jnp.minimum(view_at + 1, ranks - 1)
    has_before = view_at > 0
    has_after = view_at < ranks - 1
    full_y = RY * ranks

    def place(z, slot, mid, low_side, high_side):
        base = z * WY * SLOT + slot
        rows[pl.ds(base, REACH, stride=SLOT), :] = jnp.where(has_before, low_side[RY - REACH :], 0.0)
        rows[pl.ds(base + REACH * SLOT, RY, stride=SLOT), :] = mid
        rows[pl.ds(base + (REACH + RY) * SLOT, REACH, stride=SLOT), :] = jnp.where(
            has_after, high_side[:REACH], 0.0
        )

    for c in range(10):
        slot = c if c < 5 else c + 3
        mid = packed[view_at, c * 32 : c * 32 + 32, :].astype(F32)
        low_side = packed[before, c * 32 : c * 32 + 32, :].astype(F32)
        high_side = packed[after, c * 32 : c * 32 + 32, :].astype(F32)
        for z in range(CZ):
            cut = slice(z * RY, z * RY + RY)
            place(z, slot, mid[cut], low_side[cut], high_side[cut])
    for z in range(CZ):
        at = lambda rank: field[pl.ds(pl.multiple_of(z * full_y + rank * RY, RY), RY), :]
        place(z, 5, at(view_at), at(before), at(after))
    out[...] = rows[...].reshape(out.shape).astype(BF16)


def lane_masks(shape):
    lane = lax.broadcasted_iota(jnp.int32, shape, 1)
    return lane == 0, lane == LANES - 1


def shifted(value, first, last):
    left = jnp.where(first, 0.0, pltpu.roll(value, 1, 1))
    right = jnp.where(last, 0.0, pltpu.roll(value, LANES - 1, 1))
    return left, value, right


def shift_sum(taps, first, last):
    step = taps.shape[0] // 3
    left = jnp.where(first, 0.0, pltpu.roll(taps[:step], 1, 1))
    right = jnp.where(last, 0.0, pltpu.roll(taps[2 * step :], LANES - 1, 1))
    return taps[step : 2 * step] + left + right


def window(ref, width, z, y):
    sides = []
    for ahead in range(2):
        sides.append(
            jnp.concatenate(
                [ref[(z + a) * width + y + ahead + b] for a in range(3) for b in range(3)], axis=0
            )
        )
    return jnp.concatenate(sides, axis=1)


def side_matrix():
    row = lax.broadcasted_iota(jnp.int32, (LANES, 2 * LANES), 0)
    col = lax.broadcasted_iota(jnp.int32, (LANES, 2 * LANES), 1)
    source = jnp.where(col < LANES, col - 1, col - LANES + 1)
    source = jnp.where(source < LANES, source, -1)
    return jnp.where(row == source, 1.0, 0.0).astype(BF16)


def pipelined(count, multiply, finish, first_buf, second_buf):
    multiply(0, first_buf)

    def step(i, carry):
        multiply(2 * i + 1, second_buf)
        finish(2 * i, first_buf)
        multiply(2 * i + 2, first_buf)
        finish(2 * i + 1, second_buf)
        return carry

    lax.fori_loop(0, count // 2 - 1, step, 0)
    multiply(count - 1, second_buf)
    finish(count - 2, first_buf)
    finish(count - 1, second_buf)


def net_kernel(
    meta, prev, here, following, cot, w_in, w_mid, w_mid_flip, w_first_flip,
    d_primal, strip, packed,
    grads, ends_grad, mid_grad, buf_a, buf_b, box, slope, dz_two, z_one, z_two, da_two, da_one, dx,
):
    slab_at, view_at, slabs, ranks = meta[0], meta[1], meta[2], meta[3]
    sides = side_matrix()
    per = CZ * WY
    has = (slab_at > 0, None, slab_at < slabs - 1)
    for part, source in enumerate((prev, here, following)):
        for at in range(0, per, WY):
            rows = source[at : at + WY]
            if has[part] is not None:
                rows = jnp.where(has[part], rows, jnp.zeros_like(rows))
            both = jnp.dot(
                rows.reshape(WY * SLOT, LANES), sides, preferred_element_type=F32
            ).astype(BF16)
            to = slice(part * per + at, part * per + at + WY)
            box[to, 0:SLOT, :] = both[:, :LANES].reshape(WY, SLOT, LANES)
            box[to, SLOT : 2 * SLOT, :] = rows
            box[to, 2 * SLOT : 3 * SLOT, :] = both[:, LANES:].reshape(WY, SLOT, LANES)
    first, last = lane_masks((HID, LANES))
    z_start, y_start = slab_at * CZ, view_at * RY
    z_end, y_end = slabs * CZ, ranks * RY

    def inside(z, y, reach):
        zz, yy = z_start - reach + z, y_start - reach + y
        return (zz >= 0) & (zz < z_end) & (yy >= 0) & (yy < y_end)

    def sigmoid(value):
        return 0.5 * jnp.tanh(0.5 * value) + 0.5

    depth3, rows3 = CZ + 6, RY + 6
    depth2, rows2 = CZ + 4, RY + 4
    depth1, rows1 = CZ + 2, RY + 2

    def times(weights, source, width, rows):
        def multiply(z, buf):
            for y in range(0, rows, 2):
                buf[y // 2, 0 : weights.shape[0], :] = jnp.dot(
                    weights[...], window(source, width, z, y), preferred_element_type=F32
                )

        return multiply

    def finish_one(z, buf):
        for y in range(rows3):
            half = slice((y % 2) * LANES, (y % 2 + 1) * LANES)
            value = buf[y // 2, 0:HID, half]
            sig = sigmoid(value)
            at = z * rows3 + y
            z_one[at] = jnp.where(inside(z, y, 3), value * sig, 0.0).astype(BF16)
            slope[at] = sig * (1.0 + value * (1.0 - sig))
            dz_two[at] = buf[y // 2, HID : 2 * HID, half]

    pipelined(depth3, times(w_in, box, WY, rows3), finish_one, buf_a, buf_b)

    def finish_two(z, buf):
        for y in range(rows2):
            half = slice((y % 2) * LANES, (y % 2 + 1) * LANES)
            value = shift_sum(buf[y // 2, 0 : 3 * HID, half], first, last)
            sig = sigmoid(value)
            at = z * rows2 + y
            z_two[at] = (value * sig).astype(BF16)
            grad = dz_two[(z + 1) * rows3 + y + 1] * (sig * (1.0 + value * (1.0 - sig)))
            da_two[at] = jnp.where(inside(z, y, 2), grad, 0.0).astype(BF16)

    pipelined(depth2, times(w_mid, z_one, rows3, rows2), finish_two, buf_a, buf_b)

    def finish_back(z, buf):
        for y in range(rows1):
            half = slice((y % 2) * LANES, (y % 2 + 1) * LANES)
            value = shift_sum(buf[y // 2, 0 : 3 * HID, half], first, last)
            grad = value * slope[(z + 2) * rows3 + y + 2]
            da_one[z * rows1 + y] = jnp.where(inside(z, y, 1), grad, 0.0).astype(BF16)

    pipelined(depth1, times(w_mid_flip, da_two, rows2, rows1), finish_back, buf_a, buf_b)

    first8, last8 = lane_masks((8, LANES))
    ends_grad[...] = jnp.zeros(ends_grad.shape, F32)
    mid_grad[...] = jnp.zeros(mid_grad.shape, F32)
    contract = (((1,), (1,)), ((), ()))

    def layer_out(z, carry):
        for y in range(0, RY, 2):
            taps = jnp.dot(w_first_flip[...], window(da_one, rows1, z, y), preferred_element_type=F32)
            for s in range(2):
                at = pl.multiple_of((z * RY + y + s) * 8, 8)
                dx[pl.ds(at, 8), :] = shift_sum(taps[:, s * LANES : (s + 1) * LANES], first8, last8)
        inner = z_one[pl.ds((z + 3) * rows3 + 3, RY)]
        both = jnp.dot(
            inner.reshape(RY * HID, LANES), sides, preferred_element_type=F32
        ).astype(BF16)
        ends = jnp.concatenate(
            [
                jnp.concatenate(
                    [da_one[(z + 1) * rows1 + y + 1], z_two[(z + 2) * rows2 + y + 2]], axis=0
                )
                for y in range(RY)
            ],
            axis=1,
        )
        mids = jnp.concatenate(
            [
                jnp.concatenate(
                    [
                        both[y * HID : (y + 1) * HID, LANES:],
                        inner[y],
                        both[y * HID : (y + 1) * HID, :LANES],
                    ],
                    axis=0,
                )
                for y in range(RY)
            ],
            axis=1,
        )
        low = jnp.concatenate([window(box, WY, z + 3, y + 3) for y in range(0, RY, 2)], axis=1)
        mid = jnp.concatenate([window(da_two, rows2, z + 1, y + 1) for y in range(0, RY, 2)], axis=1)
        ends_grad[...] += lax.dot_general(low, ends, contract, preferred_element_type=F32)
        mid_grad[...] += lax.dot_general(mid, mids, contract, preferred_element_type=F32)
        return carry

    lax.fori_loop(0, CZ, layer_out, 0)

    for z in range(CZ):
        for c in range(5):
            d_primal[c, z] = cot[c, z] + dx[pl.ds(z * RY * 8 + c, RY, stride=8), :]
        strip[z * RY : (z + 1) * RY, :] = dx[pl.ds(z * RY * 8 + 5, RY, stride=8), :]
    grads[...] = jnp.zeros(grads.shape, F32)
    grads[0:288, 0 : 3 * HID] = mid_grad[...]
    for tap in range(9):
        for shift in range(3):
            at = (tap * 3 + shift) * SLOT
            to = 288 + tap * SLOT
            cut = slice(shift * HID, (shift + 1) * HID)
            grads[to : to + 8, cut] = ends_grad[at : at + 8, 0:HID]
            grads[to + 8 : to + 16, cut] = ends_grad[at + 8 : at + 16, HID : 2 * HID]
    packed[0 : grads.shape[0], :] = grads[...].astype(BF16)
    packed[grads.shape[0] :, :] = jnp.zeros((packed.shape[0] - grads.shape[0], LANES), BF16)


def dual_kernel(meta, strips, tiles, foots, prints, out, codes):
    view_at = meta[0]
    foot_count = prints.shape[0]
    ranks = strips.shape[0]
    views = tiles.shape[0] // 2 // ranks
    own = pl.ds(pl.multiple_of(view_at * views * 2, views * 2), views * 2)
    codes[...] = (tiles[own, :] * foot_count + foots[own, :]).astype(F32)
    taps = [codes[pl.ds(k, views, stride=2), :] for k in range(2)]
    pieces = [strips[d].astype(F32) for d in range(ranks)]
    field = jnp.concatenate(
        [pieces[d][z * RY : (z + 1) * RY] for z in range(CZ) for d in range(ranks)], axis=0
    ).astype(BF16)
    total = jnp.zeros((DTL * views, LANES), F32)
    contract = (((1,), (1,)), ((), ()))
    for o in range(foot_count):
        counts = jnp.concatenate(
            [
                sum(jnp.where(tap == float(g * foot_count + o), 1.0, 0.0) for tap in taps)
                for g in range(DTL)
            ],
            axis=0,
        ).astype(BF16)
        part = jnp.dot(counts, field, preferred_element_type=F32)
        high = part.astype(BF16)
        low = (part - high.astype(F32)).astype(BF16)
        both = lax.dot_general(
            jnp.concatenate([high, low], axis=0), prints[o], contract, preferred_element_type=F32
        )
        total = total + both[: DTL * views] + both[DTL * views :]
    for g in range(DTL):
        out[pl.ds(g, views, stride=DTL), :] = total[g * views : (g + 1) * views]


def sum_kernel(per, shares, out):
    block = max(per, 8)
    total = shares[...].astype(F32).reshape(shares.shape[0] // block, block, LANES).sum(axis=0)
    step = per
    while step < block:
        total = total + pltpu.roll(total, step, 0)
        step *= 2
    while total.shape[0] < 16:
        total = jnp.concatenate([total, total], axis=0)
    total = total.astype(BF16)
    for at in range(0, out.shape[0], total.shape[0]):
        out[at : at + total.shape[0], :] = total


def sum_call(per):
    def kernel(*refs):
        sum_kernel(per, *refs)

    return kernel


def split_kernel(scale, packed, d_first, d_middle, d_last):
    values = packed[0:432, :].astype(F32) * scale
    for shift in range(3):
        moved = values if shift == 0 else pltpu.roll(values, LANES - shift * HID, 1)
        for a in range(3):
            for b in range(3):
                tap = a * 3 + b
                d_middle[2 - a, 2 - b, 2 - shift] = moved[tap * HID : (tap + 1) * HID, :HID]
                at = 288 + tap * SLOT
                d_first[a, b, shift] = moved[at : at + 6, :HID]
                d_last[2 - a, 2 - b, :, 2 - shift, :] = moved[at + 8 : at + 13, :HID]


def split_call(scale):
    def kernel(*refs):
        split_kernel(scale, *refs)

    return kernel


def flipped(kernel):
    return kernel[::-1, ::-1, ::-1].transpose(0, 1, 2, 4, 3)


def by_taps(kernel, shift):
    o, i = kernel.shape[3], kernel.shape[4]
    kernel = jnp.pad(kernel, ((0, 0),) * 4 + ((shift, SLOT - i - shift),))
    return kernel.transpose(3, 0, 1, 2, 4).reshape(o, 27 * SLOT)


def by_rows(kernel, inputs_to, outputs_to):
    o, i = kernel.shape[3], kernel.shape[4]
    kernel = jnp.pad(
        kernel, ((0, 0), (0, 0), (0, 0), (0, outputs_to - o), (0, inputs_to - i))
    )
    return kernel.transpose(2, 3, 0, 1, 4).reshape(3 * outputs_to, 9 * inputs_to)


def shards(
    primal, dual, footprints, tile_index, footprint_offset, w_first, w_middle, w_last, cotangent
):
    views_here, det_tiles, bins = dual.shape
    all_views, tiles_here, taps = tile_index.shape
    ranks = lax.axis_size("view")
    slabs = lax.axis_size("slab")
    devices = ranks * slabs
    view_at = lax.axis_index("view")
    slab_at = lax.axis_index("slab")
    meta = jnp.stack([view_at]).astype(jnp.int32)
    meta_net = jnp.stack([slab_at, view_at, slabs, ranks]).astype(jnp.int32)
    flat = lambda idx: idx.transpose(0, 2, 1).reshape(all_views * taps, tiles_here)
    tiles, foots = flat(tile_index), flat(footprint_offset)

    packed = pl.pallas_call(
        pack_kernel,
        out_shape=jax.ShapeDtypeStruct((320 + views_here * det_tiles, LANES), BF16),
        in_specs=[vmem_spec()] * 3,
        out_specs=vmem_spec(),
        compiler_params=PARAMS,
        interpret=INTERPRET,
        name="pack_inputs",
    )(
        primal.reshape(160, LANES),
        cotangent.reshape(160, LANES),
        dual.reshape(views_here * det_tiles, LANES),
    )
    packed = lax.all_gather(packed, "view", axis=0, tiled=False)

    here = pl.pallas_call(
        gather_kernel,
        out_shape=jax.ShapeDtypeStruct((CZ * WY, SLOT, LANES), BF16),
        in_specs=[smem_spec()] + [vmem_spec()] * 4,
        out_specs=vmem_spec(),
        scratch_shapes=[
            pltpu.VMEM((all_views * taps, tiles_here), F32),
            pltpu.VMEM((all_views * det_tiles, LANES), F32),
            pltpu.VMEM((tiles_here, LANES), F32),
            pltpu.VMEM((CZ * WY * SLOT, LANES), F32),
        ],
        compiler_params=PARAMS,
        interpret=INTERPRET,
        name="box_rows",
    )(meta, packed, tiles, foots, footprints)

    prev = lax.ppermute(here, "slab", [(i, (i + 1) % slabs) for i in range(slabs)])
    following = lax.ppermute(here, "slab", [((i + 1) % slabs, i) for i in range(slabs)])

    w_in = jnp.concatenate([by_taps(w_first, 0), by_taps(flipped(w_last), 8)], axis=0)
    w_mid = by_rows(w_middle, HID, HID)
    w_mid_flip = by_rows(flipped(w_middle), HID, HID)
    w_first_flip = by_rows(flipped(w_first), HID, 8)

    rows3, rows2, rows1 = 140, 96, 60
    d_primal, strip, grads = pl.pallas_call(
        net_kernel,
        out_shape=(
            jax.ShapeDtypeStruct(primal.shape, F32),
            jax.ShapeDtypeStruct((CZ * RY, LANES), F32),
            jax.ShapeDtypeStruct((2 * devices if devices >= 256 else 32 * devices, LANES), BF16),
        ),
        in_specs=[smem_spec()] + [vmem_spec()] * 8,
        out_specs=(vmem_spec(),) * 3,
        scratch_shapes=[
            pltpu.VMEM((432, LANES), F32),
            pltpu.VMEM((27 * SLOT, 2 * HID), F32),
            pltpu.VMEM((288, 3 * HID), F32),
            pltpu.VMEM((7, 3 * HID, 2 * LANES), F32),
            pltpu.VMEM((7, 3 * HID, 2 * LANES), F32),
            pltpu.VMEM((3 * CZ * WY, 3 * SLOT, LANES), BF16),
            pltpu.VMEM((rows3, HID, LANES), F32),
            pltpu.VMEM((rows3, HID, LANES), F32),
            pltpu.VMEM((rows3, HID, LANES), BF16),
            pltpu.VMEM((rows2, HID, LANES), BF16),
            pltpu.VMEM((rows2, HID, LANES), BF16),
            pltpu.VMEM((rows1, HID, LANES), BF16),
            pltpu.VMEM((CZ * RY * 8, LANES), F32),
        ],
        compiler_params=PARAMS,
        interpret=INTERPRET,
        name="net_box",
    )(meta_net, prev, here, following, cotangent, w_in, w_mid, w_mid_flip, w_first_flip)

    strip = strip.astype(BF16)
    ring = lambda step: [(i, (i + step) % ranks) for i in range(ranks)]
    others = [lax.ppermute(strip, "view", ring(step)) for step in range(1, ranks)]

    both = ("slab", "view")
    per = grads.shape[0] // devices
    shares = lax.all_to_all(grads.reshape(devices, per, LANES), both, 0, 0, tiled=True)
    summed = pl.pallas_call(
        sum_call(per),
        out_shape=jax.ShapeDtypeStruct(grads.shape, BF16),
        in_specs=[vmem_spec()],
        out_specs=vmem_spec(),
        compiler_params=PARAMS,
        interpret=INTERPRET,
        name="sum_shares",
    )(shares.reshape(grads.shape))
    whole = lax.all_to_all(
        summed.reshape(shares.shape), both, 0, 0, tiled=True
    ).reshape(grads.shape)

    arrived = jnp.stack([strip] + others)
    order = (view_at - jnp.arange(ranks)) % ranks
    strips = jnp.take(arrived, order, axis=0)
    d_dual = pl.pallas_call(
        dual_kernel,
        out_shape=jax.ShapeDtypeStruct((views_here * det_tiles, LANES), F32),
        in_specs=[smem_spec()] + [vmem_spec()] * 4,
        out_specs=vmem_spec(),
        scratch_shapes=[pltpu.VMEM((views_here * taps, tiles_here), F32)],
        compiler_params=PARAMS,
        interpret=INTERPRET,
        name="dual_views",
    )(meta, strips, tiles, foots, footprints)

    full = slabs * CZ * ranks * RY * LANES
    d_first, d_middle, d_last = pl.pallas_call(
        split_call(1.0 / math.sqrt(full)),
        out_shape=(
            jax.ShapeDtypeStruct((3, 3, 3, 6, HID), F32),
            jax.ShapeDtypeStruct((3, 3, 3, HID, HID), F32),
            jax.ShapeDtypeStruct((3, 3, 5, 3, HID), F32),
        ),
        in_specs=[vmem_spec()],
        out_specs=(vmem_spec(),) * 3,
        compiler_params=PARAMS,
        interpret=INTERPRET,
        name="split_grads",
    )(whole)
    return (
        d_primal,
        d_dual.reshape(dual.shape),
        d_first.transpose(0, 1, 2, 4, 3),
        d_middle,
        d_last.transpose(0, 1, 3, 2, 4),
    )


def solution(mesh):
    placed = (
        P(None, "slab", "view", None),
        P("view", "slab", None),
        P(),
        P(None, "slab", None),
        P(None, "slab", None),
        P(),
        P(),
        P(),
        P(None, "slab", "view", None),
    )
    return jax.shard_map(
        shards,
        mesh=mesh,
        in_specs=placed,
        out_specs=(P(None, "slab", "view", None), P("view", "slab", None), P(), P(), P()),
        check_vma=False,
    )
```

```python
import math

import jax
import jax.numpy as jnp
from jax import lax
from jax.experimental import pallas as pl
from jax.experimental.pallas import tpu as pltpu
from jax.sharding import PartitionSpec as P

F32 = jnp.float32
BF16 = jnp.bfloat16
INTERPRET = False
PARAMS = pltpu.CompilerParams(vmem_limit_bytes=48 << 20)

CZ = 4
RY = 8
REACH = 4
WY = RY + 2 * REACH
LANES = 128
HID = 32
SLOT = 16
DTL = 4
SENT = 11


def smem_spec():
    return pl.BlockSpec(memory_space=pltpu.SMEM)


def vmem_spec():
    return pl.BlockSpec(memory_space=pltpu.VMEM)


def pack_kernel(primal, cotangent, dual, out, primal_in, cotangent_in, dual_in, sems):
    copies = [
        pltpu.make_async_copy(primal, primal_in, sems.at[0]),
        pltpu.make_async_copy(cotangent, cotangent_in, sems.at[1]),
        pltpu.make_async_copy(dual, dual_in, sems.at[2]),
    ]
    for copy in copies:
        copy.start()
    for copy in copies:
        copy.wait()
    out[0:160, :] = primal_in[...].astype(BF16)
    out[160:320, :] = cotangent_in[...].astype(BF16)
    out[320:, :] = dual_in[...]


def gather_kernel(meta, packed, tiles, foots, prints, out, codes, duals, field, rows):
    view_at = meta[0]
    foot_count = prints.shape[0]
    views = tiles.shape[0] // 2
    codes[...] = (tiles[...] * foot_count + foots[...]).astype(F32)
    by_tap = jnp.concatenate(
        [codes[pl.ds(0, views, stride=2), :], codes[pl.ds(1, views, stride=2), :]], axis=0
    )
    by_tile = by_tap.T
    ranks = packed.shape[0]
    local = views // ranks * DTL
    for d in range(ranks):
        duals[d * local : (d + 1) * local, :] = packed[d, 320 : 320 + local, :].astype(F32)
    stack = []
    for g in range(DTL):
        one = duals[pl.ds(g, views, stride=DTL), :].astype(BF16)
        stack += [one, one]
    dual_rows = jnp.concatenate(stack, axis=0)
    back = jnp.zeros((by_tile.shape[0], LANES), F32)
    for o in range(foot_count):
        counts = jnp.concatenate(
            [
                jnp.where(by_tile == float(g * foot_count + o), 1.0, 0.0).astype(BF16)
                for g in range(DTL)
            ],
            axis=1,
        )
        part = jnp.dot(counts, dual_rows, preferred_element_type=F32)
        high = part.astype(BF16)
        low = (part - high.astype(F32)).astype(BF16)
        back = back + jnp.dot(high, prints[o], preferred_element_type=F32)
        back = back + jnp.dot(low, prints[o], preferred_element_type=F32)
    field[...] = back

    before = jnp.maximum(view_at - 1, 0)
    after = jnp.minimum(view_at + 1, ranks - 1)
    has_before = view_at > 0
    has_after = view_at < ranks - 1
    full_y = RY * ranks

    def place(z, slot, mid, low_side, high_side):
        base = z * WY * SENT + slot
        rows[pl.ds(base, REACH, stride=SENT), :] = jnp.where(has_before, low_side[RY - REACH :], 0.0)
        rows[pl.ds(base + REACH * SENT, RY, stride=SENT), :] = mid
        rows[pl.ds(base + (REACH + RY) * SENT, REACH, stride=SENT), :] = jnp.where(
            has_after, high_side[:REACH], 0.0
        )

    for c in range(10):
        slot = c if c < 5 else c + 1
        mid = packed[view_at, c * 32 : c * 32 + 32, :].astype(F32)
        low_side = packed[before, c * 32 : c * 32 + 32, :].astype(F32)
        high_side = packed[after, c * 32 : c * 32 + 32, :].astype(F32)
        for z in range(CZ):
            cut = slice(z * RY, z * RY + RY)
            place(z, slot, mid[cut], low_side[cut], high_side[cut])
    for z in range(CZ):
        at = lambda rank: field[pl.ds(pl.multiple_of(z * full_y + rank * RY, RY), RY), :]
        place(z, 5, at(view_at), at(before), at(after))
    out[...] = rows[...].astype(BF16)


def lane_masks(shape):
    lane = lax.broadcasted_iota(jnp.int32, shape, 1)
    return lane == 0, lane == LANES - 1


def shifted(value, first, last):
    left = jnp.where(first, 0.0, pltpu.roll(value, 1, 1))
    right = jnp.where(last, 0.0, pltpu.roll(value, LANES - 1, 1))
    return left, value, right


def shift_sum(taps, first, last):
    step = taps.shape[0] // 3
    left = jnp.where(first, 0.0, pltpu.roll(taps[:step], 1, 1))
    right = jnp.where(last, 0.0, pltpu.roll(taps[2 * step :], LANES - 1, 1))
    return taps[step : 2 * step] + left + right


def window(ref, width, z, y):
    sides = []
    for ahead in range(2):
        sides.append(
            jnp.concatenate(
                [ref[(z + a) * width + y + ahead + b] for a in range(3) for b in range(3)], axis=0
            )
        )
    return jnp.concatenate(sides, axis=1)


def side_matrix():
    row = lax.broadcasted_iota(jnp.int32, (LANES, 2 * LANES), 0)
    col = lax.broadcasted_iota(jnp.int32, (LANES, 2 * LANES), 1)
    source = jnp.where(col < LANES, col - 1, col - LANES + 1)
    source = jnp.where(source < LANES, source, -1)
    return jnp.where(row == source, 1.0, 0.0).astype(BF16)


def spread_matrix():
    shape = (WY * SLOT, WY * SENT)
    row = lax.broadcasted_iota(jnp.int32, shape, 0)
    col = lax.broadcasted_iota(jnp.int32, shape, 1)
    slot = row & (SLOT - 1)
    channel = jnp.where(slot < 6, slot, jnp.where((slot >= 8) & (slot < 13), slot - 2, -WY * SENT))
    return jnp.where(col == (row >> 4) * SENT + channel, 1.0, 0.0).astype(BF16)


def pipelined(count, multiply, finish, first_buf, second_buf):
    multiply(0, first_buf)

    bufs = (first_buf, second_buf)
    for z in range(1, count):
        multiply(z, bufs[z % 2])
        finish(z - 1, bufs[1 - z % 2])
    finish(count - 1, bufs[1 - count % 2])


def net_kernel(
    meta, paired, here, crossed, w_in, w_mid, w_mid_flip,
    da_one, packed,
    grads, ends_grad, mid_grad, buf_a, buf_b, box, slope, dz_two, z_one, z_two, da_two,
):
    slab_at, view_at, slabs, ranks = meta[0], meta[1], meta[2], meta[3]
    sides = side_matrix()
    spread = spread_matrix()
    per = CZ * WY
    odd = slab_at % 2 == 1
    has_prev, has_next = slab_at > 0, slab_at < slabs - 1
    for part in range(3):
        for z in range(CZ):
            cut = slice(z * WY * SENT, (z + 1) * WY * SENT)
            if part == 1:
                rows = here[cut]
            else:
                towards, away = paired[cut], crossed[cut]
                rows = jnp.where(odd, towards, away) if part == 0 else jnp.where(odd, away, towards)
                rows = jnp.where(has_next if part else has_prev, rows, jnp.zeros_like(rows))
            rows = jnp.dot(spread, rows, preferred_element_type=F32).astype(BF16)
            both = jnp.dot(rows, sides, preferred_element_type=F32).astype(BF16)
            to = slice(part * per + z * WY, part * per + (z + 1) * WY)
            box[to, 0:SLOT, :] = both[:, :LANES].reshape(WY, SLOT, LANES)
            box[to, SLOT : 2 * SLOT, :] = rows.reshape(WY, SLOT, LANES)
            box[to, 2 * SLOT : 3 * SLOT, :] = both[:, LANES:].reshape(WY, SLOT, LANES)
    first, last = lane_masks((HID, LANES))
    z_start, y_start = slab_at * CZ, view_at * RY
    z_end, y_end = slabs * CZ, ranks * RY

    def inside(z, y, reach):
        zz, yy = z_start - reach + z, y_start - reach + y
        return (zz >= 0) & (zz < z_end) & (yy >= 0) & (yy < y_end)

    def sigmoid(value):
        return 0.5 * jnp.tanh(0.5 * value) + 0.5

    depth3, rows3 = CZ + 6, RY + 6
    depth2, rows2 = CZ + 4, RY + 4
    depth1, rows1 = CZ + 2, RY + 2

    def times(weights, source, width, rows):
        def multiply(z, buf):
            for y in range(0, rows, 2):
                buf[y // 2, 0 : weights.shape[0], :] = jnp.dot(
                    weights[...], window(source, width, z, y), preferred_element_type=F32
                )

        return multiply

    def finish_one(z, buf):
        for y in range(rows3):
            half = slice((y % 2) * LANES, (y % 2 + 1) * LANES)
            value = buf[y // 2, 0:HID, half]
            sig = sigmoid(value)
            at = z * rows3 + y
            z_one[at] = jnp.where(inside(z, y, 3), value * sig, 0.0).astype(BF16)
            slope[at] = sig * (1.0 + value * (1.0 - sig))
            dz_two[at] = buf[y // 2, HID : 2 * HID, half]

    pipelined(depth3, times(w_in, box, WY, rows3), finish_one, buf_a, buf_b)

    def finish_two(z, buf):
        for y in range(rows2):
            half = slice((y % 2) * LANES, (y % 2 + 1) * LANES)
            value = shift_sum(buf[y // 2, 0 : 3 * HID, half], first, last)
            sig = sigmoid(value)
            at = z * rows2 + y
            z_two[at] = (value * sig).astype(BF16)
            grad = dz_two[(z + 1) * rows3 + y + 1] * (sig * (1.0 + value * (1.0 - sig)))
            da_two[at] = jnp.where(inside(z, y, 2), grad, 0.0).astype(BF16)

    pipelined(depth2, times(w_mid, z_one, rows3, rows2), finish_two, buf_a, buf_b)

    def finish_back(z, buf):
        for y in range(rows1):
            half = slice((y % 2) * LANES, (y % 2 + 1) * LANES)
            value = shift_sum(buf[y // 2, 0 : 3 * HID, half], first, last)
            grad = value * slope[(z + 2) * rows3 + y + 2]
            da_one[z * rows1 + y] = jnp.where(inside(z, y, 1), grad, 0.0).astype(BF16)

    pipelined(depth1, times(w_mid_flip, da_two, rows2, rows1), finish_back, buf_a, buf_b)

    ends_grad[...] = jnp.zeros(ends_grad.shape, F32)
    mid_grad[...] = jnp.zeros(mid_grad.shape, F32)
    contract = (((1,), (1,)), ((), ()))

    def layer_out(z, carry):
        inner = z_one[pl.ds((z + 3) * rows3 + 3, RY)]
        both = jnp.dot(
            inner.reshape(RY * HID, LANES), sides, preferred_element_type=F32
        ).astype(BF16)
        ends = jnp.concatenate(
            [
                jnp.concatenate(
                    [da_one[(z + 1) * rows1 + y + 1], z_two[(z + 2) * rows2 + y + 2]], axis=0
                )
                for y in range(RY)
            ],
            axis=1,
        )
        mids = jnp.concatenate(
            [
                jnp.concatenate(
                    [
                        both[y * HID : (y + 1) * HID, LANES:],
                        inner[y],
                        both[y * HID : (y + 1) * HID, :LANES],
                    ],
                    axis=0,
                )
                for y in range(RY)
            ],
            axis=1,
        )
        low = jnp.concatenate([window(box, WY, z + 3, y + 3) for y in range(0, RY, 2)], axis=1)
        mid = jnp.concatenate([window(da_two, rows2, z + 1, y + 1) for y in range(0, RY, 2)], axis=1)
        ends_grad[...] += lax.dot_general(low, ends, contract, preferred_element_type=F32)
        mid_grad[...] += lax.dot_general(mid, mids, contract, preferred_element_type=F32)
        return carry

    lax.fori_loop(0, CZ, layer_out, 0)

    grads[...] = jnp.zeros(grads.shape, F32)
    grads[0:288, 0 : 3 * HID] = mid_grad[...]
    for tap in range(9):
        for shift in range(3):
            at = (tap * 3 + shift) * SLOT
            to = 288 + tap * SLOT
            cut = slice(shift * HID, (shift + 1) * HID)
            grads[to : to + 8, cut] = ends_grad[at : at + 8, 0:HID]
            grads[to + 8 : to + 16, cut] = ends_grad[at + 8 : at + 16, HID : 2 * HID]
    packed[0 : grads.shape[0], :] = grads[...].astype(BF16)
    packed[grads.shape[0] :, :] = jnp.zeros((packed.shape[0] - grads.shape[0], LANES), BF16)


def last_kernel(da_one, cot, w_first_flip, d_primal, strip, dx):
    rows1 = RY + 2
    first, last = lane_masks((8, LANES))
    for z in range(CZ):
        for y in range(0, RY, 2):
            taps = jnp.dot(w_first_flip[...], window(da_one, rows1, z, y), preferred_element_type=F32)
            for s in range(2):
                at = (z * RY + y + s) * 8
                dx[at : at + 8, :] = shift_sum(taps[:, s * LANES : (s + 1) * LANES], first, last)
    fields = []
    for z in range(CZ):
        for c in range(5):
            d_primal[c, z] = cot[c, z] + dx[pl.ds(z * RY * 8 + c, RY, stride=8), :]
        fields.append(dx[pl.ds(z * RY * 8 + 5, RY, stride=8), :])
    strip[...] = jnp.concatenate(fields, axis=0).astype(BF16)


def dual_kernel(meta, strips, tiles, foots, prints, out, codes):
    view_at = meta[0]
    foot_count = prints.shape[0]
    ranks = strips.shape[0]
    views = tiles.shape[0] // 2 // ranks
    own = pl.ds(pl.multiple_of(view_at * views * 2, views * 2), views * 2)
    codes[...] = (tiles[own, :] * foot_count + foots[own, :]).astype(F32)
    taps = [codes[pl.ds(k, views, stride=2), :] for k in range(2)]
    pieces = [strips[d].astype(F32) for d in range(ranks)]
    field = jnp.concatenate(
        [pieces[d][z * RY : (z + 1) * RY] for z in range(CZ) for d in range(ranks)], axis=0
    ).astype(BF16)
    total = jnp.zeros((DTL * views, LANES), F32)
    contract = (((1,), (1,)), ((), ()))
    for o in range(foot_count):
        counts = jnp.concatenate(
            [
                sum(jnp.where(tap == float(g * foot_count + o), 1.0, 0.0) for tap in taps)
                for g in range(DTL)
            ],
            axis=0,
        ).astype(BF16)
        part = jnp.dot(counts, field, preferred_element_type=F32)
        high = part.astype(BF16)
        low = (part - high.astype(F32)).astype(BF16)
        both = lax.dot_general(
            jnp.concatenate([high, low], axis=0), prints[o], contract, preferred_element_type=F32
        )
        total = total + both[: DTL * views] + both[DTL * views :]
    for g in range(DTL):
        out[pl.ds(g, views, stride=DTL), :] = total[g * views : (g + 1) * views]


def sum_kernel(per, shares, out):
    block = max(per, 8)
    total = shares[...].astype(F32).reshape(shares.shape[0] // block, block, LANES).sum(axis=0)
    step = per
    while step < block:
        total = total + pltpu.roll(total, step, 0)
        step *= 2
    while total.shape[0] < 16:
        total = jnp.concatenate([total, total], axis=0)
    total = total.astype(BF16)
    for at in range(0, out.shape[0], total.shape[0]):
        out[at : at + total.shape[0], :] = total


def sum_call(per):
    def kernel(*refs):
        sum_kernel(per, *refs)

    return kernel


def split_kernel(scale, packed, d_first, d_middle, d_last):
    values = packed[0:432, :].astype(F32) * scale
    for shift in range(3):
        moved = values if shift == 0 else pltpu.roll(values, LANES - shift * HID, 1)
        for a in range(3):
            for b in range(3):
                tap = a * 3 + b
                d_middle[2 - a, 2 - b, 2 - shift] = moved[tap * HID : (tap + 1) * HID, :HID]
                at = 288 + tap * SLOT
                d_first[a, b, shift] = moved[at : at + 6, :HID]
                d_last[2 - a, 2 - b, :, 2 - shift, :] = moved[at + 8 : at + 13, :HID]


def split_call(scale):
    def kernel(*refs):
        split_kernel(scale, *refs)

    return kernel


def flipped(kernel):
    return kernel[::-1, ::-1, ::-1].transpose(0, 1, 2, 4, 3)


def by_taps(kernel, shift):
    o, i = kernel.shape[3], kernel.shape[4]
    kernel = jnp.pad(kernel, ((0, 0),) * 4 + ((shift, SLOT - i - shift),))
    return kernel.transpose(3, 0, 1, 2, 4).reshape(o, 27 * SLOT)


def by_rows(kernel, inputs_to, outputs_to):
    o, i = kernel.shape[3], kernel.shape[4]
    kernel = jnp.pad(
        kernel, ((0, 0), (0, 0), (0, 0), (0, outputs_to - o), (0, inputs_to - i))
    )
    return kernel.transpose(2, 3, 0, 1, 4).reshape(3 * outputs_to, 9 * inputs_to)


def shards(
    primal, dual, footprints, tile_index, footprint_offset, w_first, w_middle, w_last, cotangent
):
    views_here, det_tiles, bins = dual.shape
    all_views, tiles_here, taps = tile_index.shape
    ranks = lax.axis_size("view")
    slabs = lax.axis_size("slab")
    devices = ranks * slabs
    view_at = lax.axis_index("view")
    slab_at = lax.axis_index("slab")
    meta = jnp.stack([view_at]).astype(jnp.int32)
    meta_net = jnp.stack([slab_at, view_at, slabs, ranks]).astype(jnp.int32)
    flat = lambda idx: idx.transpose(0, 2, 1).reshape(all_views * taps, tiles_here)
    tiles, foots = flat(tile_index), flat(footprint_offset)

    packed = pl.pallas_call(
        pack_kernel,
        out_shape=jax.ShapeDtypeStruct((320 + views_here * det_tiles, LANES), BF16),
        in_specs=[pl.BlockSpec(memory_space=pl.ANY)] * 3,
        out_specs=vmem_spec(),
        scratch_shapes=[
            pltpu.VMEM((160, LANES), F32),
            pltpu.VMEM((160, LANES), F32),
            pltpu.VMEM((views_here * det_tiles, LANES), BF16),
            pltpu.SemaphoreType.DMA((3,)),
        ],
        compiler_params=PARAMS,
        interpret=INTERPRET,
        name="pack_inputs",
    )(
        primal.reshape(160, LANES),
        cotangent.reshape(160, LANES),
        dual.reshape(views_here * det_tiles, LANES),
    )
    packed = lax.all_gather(packed, "view", axis=0, tiled=False)

    here = pl.pallas_call(
        gather_kernel,
        out_shape=jax.ShapeDtypeStruct((CZ * WY * SENT, LANES), BF16),
        in_specs=[smem_spec()] + [vmem_spec()] * 4,
        out_specs=vmem_spec(),
        scratch_shapes=[
            pltpu.VMEM((all_views * taps, tiles_here), F32),
            pltpu.VMEM((all_views * det_tiles, LANES), F32),
            pltpu.VMEM((tiles_here, LANES), F32),
            pltpu.VMEM((CZ * WY * SENT, LANES), F32),
        ],
        compiler_params=PARAMS,
        interpret=INTERPRET,
        name="box_rows",
    )(meta, packed, tiles, foots, footprints)

    inner = lambda i: i if i == 0 or i == slabs - 1 else ((i - 1) ^ 1) + 1
    paired = lax.ppermute(here, "slab", [(i, i ^ 1) for i in range(slabs)])
    crossed = lax.ppermute(here, "slab", [(i, inner(i)) for i in range(slabs)])

    w_in = jnp.concatenate([by_taps(w_first, 0), by_taps(flipped(w_last), 8)], axis=0)
    w_mid = by_rows(w_middle, HID, HID)
    w_mid_flip = by_rows(flipped(w_middle), HID, HID)
    w_first_flip = by_rows(flipped(w_first), HID, 8)

    rows3, rows2, rows1 = 140, 96, 60
    da_one, grads = pl.pallas_call(
        net_kernel,
        out_shape=(
            jax.ShapeDtypeStruct((rows1, HID, LANES), BF16),
            jax.ShapeDtypeStruct((2 * devices if devices >= 256 else 32 * devices, LANES), BF16),
        ),
        in_specs=[smem_spec()] + [vmem_spec()] * 6,
        out_specs=(vmem_spec(),) * 2,
        scratch_shapes=[
            pltpu.VMEM((432, LANES), F32),
            pltpu.VMEM((27 * SLOT, 2 * HID), F32),
            pltpu.VMEM((288, 3 * HID), F32),
            pltpu.VMEM((7, 3 * HID, 2 * LANES), F32),
            pltpu.VMEM((7, 3 * HID, 2 * LANES), F32),
            pltpu.VMEM((3 * CZ * WY, 3 * SLOT, LANES), BF16),
            pltpu.VMEM((rows3, HID, LANES), F32),
            pltpu.VMEM((rows3, HID, LANES), F32),
            pltpu.VMEM((rows3, HID, LANES), BF16),
            pltpu.VMEM((rows2, HID, LANES), BF16),
            pltpu.VMEM((rows2, HID, LANES), BF16),
        ],
        compiler_params=PARAMS,
        interpret=INTERPRET,
        name="net_box",
    )(meta_net, paired, here, crossed, w_in, w_mid, w_mid_flip)

    both = ("slab", "view")
    per = grads.shape[0] // devices
    shares = lax.all_to_all(grads.reshape(devices, per, LANES), both, 0, 0, tiled=True)

    d_primal, strip = pl.pallas_call(
        last_kernel,
        out_shape=(
            jax.ShapeDtypeStruct(primal.shape, F32),
            jax.ShapeDtypeStruct((CZ * RY, LANES), BF16),
        ),
        in_specs=[vmem_spec()] * 3,
        out_specs=(vmem_spec(),) * 2,
        scratch_shapes=[pltpu.VMEM((CZ * RY * 8, LANES), F32)],
        compiler_params=PARAMS,
        interpret=INTERPRET,
        name="last_layer",
    )(da_one, cotangent, w_first_flip)

    ring = lambda step: [(i, (i + step) % ranks) for i in range(ranks)]
    others = [lax.ppermute(strip, "view", ring(step)) for step in range(1, ranks)]

    summed = pl.pallas_call(
        sum_call(per),
        out_shape=jax.ShapeDtypeStruct(grads.shape, BF16),
        in_specs=[vmem_spec()],
        out_specs=vmem_spec(),
        compiler_params=PARAMS,
        interpret=INTERPRET,
        name="sum_shares",
    )(shares.reshape(grads.shape))
    whole = lax.all_to_all(
        summed.reshape(shares.shape), both, 0, 0, tiled=True
    ).reshape(grads.shape)

    arrived = jnp.stack([strip] + others)
    order = (view_at - jnp.arange(ranks)) % ranks
    strips = jnp.take(arrived, order, axis=0)
    d_dual = pl.pallas_call(
        dual_kernel,
        out_shape=jax.ShapeDtypeStruct((views_here * det_tiles, LANES), F32),
        in_specs=[smem_spec()] + [vmem_spec()] * 4,
        out_specs=vmem_spec(),
        scratch_shapes=[pltpu.VMEM((views_here * taps, tiles_here), F32)],
        compiler_params=PARAMS,
        interpret=INTERPRET,
        name="dual_views",
    )(meta, strips, tiles, foots, footprints)

    full = slabs * CZ * ranks * RY * LANES
    d_first, d_middle, d_last = pl.pallas_call(
        split_call(1.0 / math.sqrt(full)),
        out_shape=(
            jax.ShapeDtypeStruct((3, 3, 3, 6, HID), F32),
            jax.ShapeDtypeStruct((3, 3, 3, HID, HID), F32),
            jax.ShapeDtypeStruct((3, 3, 5, 3, HID), F32),
        ),
        in_specs=[vmem_spec()],
        out_specs=(vmem_spec(),) * 3,
        compiler_params=PARAMS,
        interpret=INTERPRET,
        name="split_grads",
    )(whole)
    return (
        d_primal,
        d_dual.reshape(dual.shape),
        d_first.transpose(0, 1, 2, 4, 3),
        d_middle,
        d_last.transpose(0, 1, 3, 2, 4),
    )


def solution(mesh):
    placed = (
        P(None, "slab", "view", None),
        P("view", "slab", None),
        P(),
        P(None, "slab", None),
        P(None, "slab", None),
        P(),
        P(),
        P(),
        P(None, "slab", "view", None),
    )
    return jax.shard_map(
        shards,
        mesh=mesh,
        in_specs=placed,
        out_specs=(P(None, "slab", "view", None), P("view", "slab", None), P(), P(), P()),
        check_vma=False,
    )
```

```python
import math

import jax
import jax.numpy as jnp
from jax import lax
from jax.experimental import pallas as pl
from jax.experimental.pallas import tpu as pltpu
from jax.sharding import PartitionSpec as P


F32 = jnp.float32
BF16 = jnp.bfloat16
INTERPRET = False
PARAMS = pltpu.CompilerParams(vmem_limit_bytes=48 << 20)

CZ = 4
RY = 8
REACH = 4
WY = RY + 2 * REACH
LANES = 128
HID = 32
SLOT = 16
DTL = 4
SENT = 11


def smem_spec():
    return pl.BlockSpec(memory_space=pltpu.SMEM)


def vmem_spec():
    return pl.BlockSpec(memory_space=pltpu.VMEM)


def in_hbm(array):
    return array if INTERPRET else pltpu.with_memory_space_constraint(array, pltpu.HBM)


def pack_kernel(primal, cotangent, dual, out, primal_in, cotangent_in, dual_in, sems):
    copies = [
        pltpu.make_async_copy(primal, primal_in, sems.at[0]),
        pltpu.make_async_copy(cotangent, cotangent_in, sems.at[1]),
        pltpu.make_async_copy(dual, dual_in, sems.at[2]),
    ]
    for copy in copies:
        copy.start()
    for copy in copies:
        copy.wait()
    out[0:160, :] = primal_in[...].astype(BF16)
    out[160:320, :] = cotangent_in[...].astype(BF16)
    out[320:, :] = dual_in[...]


def gather_kernel(meta, packed, tiles, foots, prints, out, codes, duals, field, rows):
    view_at = meta[0]
    foot_count = prints.shape[0]
    views = tiles.shape[0] // 2
    codes[...] = (tiles[...] * foot_count + foots[...]).astype(F32)
    by_tap = jnp.concatenate(
        [codes[pl.ds(0, views, stride=2), :], codes[pl.ds(1, views, stride=2), :]], axis=0
    )
    by_tile = by_tap.T
    ranks = packed.shape[0]
    local = views // ranks * DTL
    for d in range(ranks):
        duals[d * local : (d + 1) * local, :] = packed[d, 320 : 320 + local, :].astype(F32)
    stack = []
    for g in range(DTL):
        one = duals[pl.ds(g, views, stride=DTL), :].astype(BF16)
        stack += [one, one]
    dual_rows = jnp.concatenate(stack, axis=0)
    back = jnp.zeros((by_tile.shape[0], LANES), F32)
    for o in range(foot_count):
        counts = jnp.concatenate(
            [
                jnp.where(by_tile == float(g * foot_count + o), 1.0, 0.0).astype(BF16)
                for g in range(DTL)
            ],
            axis=1,
        )
        part = jnp.dot(counts, dual_rows, preferred_element_type=F32)
        high = part.astype(BF16)
        low = (part - high.astype(F32)).astype(BF16)
        back = back + jnp.dot(high, prints[o], preferred_element_type=F32)
        back = back + jnp.dot(low, prints[o], preferred_element_type=F32)
    field[...] = back

    before = jnp.maximum(view_at - 1, 0)
    after = jnp.minimum(view_at + 1, ranks - 1)
    has_before = view_at > 0
    has_after = view_at < ranks - 1
    full_y = RY * ranks

    def place(z, slot, mid, low_side, high_side):
        base = z * WY * SENT + slot
        rows[pl.ds(base, REACH, stride=SENT), :] = jnp.where(has_before, low_side[RY - REACH :], 0.0)
        rows[pl.ds(base + REACH * SENT, RY, stride=SENT), :] = mid
        rows[pl.ds(base + (REACH + RY) * SENT, REACH, stride=SENT), :] = jnp.where(
            has_after, high_side[:REACH], 0.0
        )

    for c in range(10):
        slot = c if c < 5 else c + 1
        mid = packed[view_at, c * 32 : c * 32 + 32, :].astype(F32)
        low_side = packed[before, c * 32 : c * 32 + 32, :].astype(F32)
        high_side = packed[after, c * 32 : c * 32 + 32, :].astype(F32)
        for z in range(CZ):
            cut = slice(z * RY, z * RY + RY)
            place(z, slot, mid[cut], low_side[cut], high_side[cut])
    for z in range(CZ):
        at = lambda rank: field[pl.ds(pl.multiple_of(z * full_y + rank * RY, RY), RY), :]
        place(z, 5, at(view_at), at(before), at(after))
    out[...] = rows[...].astype(BF16)


def lane_masks(shape):
    lane = lax.broadcasted_iota(jnp.int32, shape, 1)
    return lane == 0, lane == LANES - 1


def shift_sum(taps, first, last):
    step = taps.shape[0] // 3
    left = jnp.where(first, 0.0, pltpu.roll(taps[:step], 1, 1))
    right = jnp.where(last, 0.0, pltpu.roll(taps[2 * step :], LANES - 1, 1))
    return taps[step : 2 * step] + left + right


def window(ref, width, z, y):
    sides = []
    for ahead in range(2):
        sides.append(
            jnp.concatenate(
                [ref[(z + a) * width + y + ahead + b] for a in range(3) for b in range(3)], axis=0
            )
        )
    return jnp.concatenate(sides, axis=1)


def side_matrix():
    row = lax.broadcasted_iota(jnp.int32, (LANES, 2 * LANES), 0)
    col = lax.broadcasted_iota(jnp.int32, (LANES, 2 * LANES), 1)
    source = jnp.where(col < LANES, col - 1, col - LANES + 1)
    source = jnp.where(source < LANES, source, -1)
    return jnp.where(row == source, 1.0, 0.0).astype(BF16)


def spread_matrix():
    shape = (WY * SLOT, WY * SENT)
    row = lax.broadcasted_iota(jnp.int32, shape, 0)
    col = lax.broadcasted_iota(jnp.int32, shape, 1)
    slot = row & (SLOT - 1)
    channel = jnp.where(slot < 6, slot, jnp.where((slot >= 8) & (slot < 13), slot - 2, -WY * SENT))
    return jnp.where(col == (row >> 4) * SENT + channel, 1.0, 0.0).astype(BF16)


def pipelined(count, multiply, finish, first_buf, second_buf):
    multiply(0, first_buf)

    bufs = (first_buf, second_buf)
    for z in range(1, count):
        multiply(z, bufs[z % 2])
        finish(z - 1, bufs[1 - z % 2])
    finish(count - 1, bufs[1 - count % 2])


def net_kernel(
    meta, paired, here, crossed, w_in, w_mid, w_mid_flip,
    da_one, packed,
    grads, ends_grad, mid_grad, buf_a, buf_b, box, slope, dz_two, z_one, z_two, da_two,
):
    slab_at, view_at, slabs, ranks = meta[0], meta[1], meta[2], meta[3]
    sides = side_matrix()
    spread = spread_matrix()
    per = CZ * WY
    odd = slab_at % 2 == 1
    has_prev, has_next = slab_at > 0, slab_at < slabs - 1
    for part in range(3):
        for z in range(0, CZ, 2):
            pair = []
            for at in range(z, z + 2):
                cut = slice(at * WY * SENT, (at + 1) * WY * SENT)
                if part == 1:
                    rows = here[cut]
                else:
                    near, far = paired[cut], crossed[cut]
                    rows = jnp.where(odd, near, far) if part == 0 else jnp.where(odd, far, near)
                    rows = jnp.where(has_next if part else has_prev, rows, jnp.zeros_like(rows))
                pair.append(rows)
            spaced = jnp.dot(
                spread, jnp.concatenate(pair, axis=1), preferred_element_type=F32
            ).astype(BF16)
            for at in range(2):
                rows = spaced[:, at * LANES : (at + 1) * LANES]
                both = jnp.dot(rows, sides, preferred_element_type=F32).astype(BF16)
                to = slice(part * per + (z + at) * WY, part * per + (z + at + 1) * WY)
                box[to, 0:SLOT, :] = both[:, :LANES].reshape(WY, SLOT, LANES)
                box[to, SLOT : 2 * SLOT, :] = rows.reshape(WY, SLOT, LANES)
                box[to, 2 * SLOT : 3 * SLOT, :] = both[:, LANES:].reshape(WY, SLOT, LANES)
    first, last = lane_masks((HID, LANES))
    z_start, y_start = slab_at * CZ, view_at * RY
    z_end, y_end = slabs * CZ, ranks * RY

    def inside(z, y, reach):
        zz, yy = z_start - reach + z, y_start - reach + y
        return (zz >= 0) & (zz < z_end) & (yy >= 0) & (yy < y_end)

    def sigmoid(value):
        return 0.5 * jnp.tanh(0.5 * value) + 0.5

    depth3, rows3 = CZ + 6, RY + 6
    depth2, rows2 = CZ + 4, RY + 4
    depth1, rows1 = CZ + 2, RY + 2

    def times(weights, source, width, rows):
        def multiply(z, buf):
            for y in range(0, rows, 2):
                buf[y // 2, 0 : weights.shape[0], :] = jnp.dot(
                    weights[...], window(source, width, z, y), preferred_element_type=F32
                )

        return multiply

    def finish_one(z, buf):
        for y in range(rows3):
            half = slice((y % 2) * LANES, (y % 2 + 1) * LANES)
            value = buf[y // 2, 0:HID, half]
            sig = sigmoid(value)
            at = z * rows3 + y
            z_one[at] = jnp.where(inside(z, y, 3), value * sig, 0.0).astype(BF16)
            slope[at] = sig * (1.0 + value * (1.0 - sig))
            dz_two[at] = buf[y // 2, HID : 2 * HID, half]

    pipelined(depth3, times(w_in, box, WY, rows3), finish_one, buf_a, buf_b)

    def finish_two(z, buf):
        for y in range(rows2):
            half = slice((y % 2) * LANES, (y % 2 + 1) * LANES)
            value = shift_sum(buf[y // 2, 0 : 3 * HID, half], first, last)
            sig = sigmoid(value)
            at = z * rows2 + y
            z_two[at] = (value * sig).astype(BF16)
            grad = dz_two[(z + 1) * rows3 + y + 1] * (sig * (1.0 + value * (1.0 - sig)))
            da_two[at] = jnp.where(inside(z, y, 2), grad, 0.0).astype(BF16)

    pipelined(depth2, times(w_mid, z_one, rows3, rows2), finish_two, buf_a, buf_b)

    def finish_back(z, buf):
        for y in range(rows1):
            half = slice((y % 2) * LANES, (y % 2 + 1) * LANES)
            value = shift_sum(buf[y // 2, 0 : 3 * HID, half], first, last)
            grad = value * slope[(z + 2) * rows3 + y + 2]
            da_one[z * rows1 + y] = jnp.where(inside(z, y, 1), grad, 0.0).astype(BF16)

    pipelined(depth1, times(w_mid_flip, da_two, rows2, rows1), finish_back, buf_a, buf_b)

    ends_grad[...] = jnp.zeros(ends_grad.shape, F32)
    mid_grad[...] = jnp.zeros(mid_grad.shape, F32)
    contract = (((1,), (1,)), ((), ()))

    def layer_out(z, carry):
        inner = z_one[pl.ds((z + 3) * rows3 + 3, RY)]
        both = jnp.dot(
            inner.reshape(RY * HID, LANES), sides, preferred_element_type=F32
        ).astype(BF16)
        ends = jnp.concatenate(
            [
                jnp.concatenate(
                    [da_one[(z + 1) * rows1 + y + 1], z_two[(z + 2) * rows2 + y + 2]], axis=0
                )
                for y in range(RY)
            ],
            axis=1,
        )
        mids = jnp.concatenate(
            [
                jnp.concatenate(
                    [
                        both[y * HID : (y + 1) * HID, LANES:],
                        inner[y],
                        both[y * HID : (y + 1) * HID, :LANES],
                    ],
                    axis=0,
                )
                for y in range(RY)
            ],
            axis=1,
        )
        low = jnp.concatenate([window(box, WY, z + 3, y + 3) for y in range(0, RY, 2)], axis=1)
        mid = jnp.concatenate([window(da_two, rows2, z + 1, y + 1) for y in range(0, RY, 2)], axis=1)
        ends_grad[0 : 2 * HID, 0 : 27 * SLOT] += lax.dot_general(
            ends, low, contract, preferred_element_type=F32
        )
        mid_grad[...] += lax.dot_general(mid, mids, contract, preferred_element_type=F32)
        return carry

    lax.fori_loop(0, CZ, layer_out, 0)

    grads[...] = jnp.zeros(grads.shape, F32)
    grads[0:288, 0 : 3 * HID] = mid_grad[...]
    turned = ends_grad[...].T
    for tap in range(9):
        for shift in range(3):
            at = (tap * 3 + shift) * SLOT
            to = 288 + tap * SLOT
            cut = slice(shift * HID, (shift + 1) * HID)
            grads[to : to + 8, cut] = turned[at : at + 8, 0:HID]
            grads[to + 8 : to + 16, cut] = turned[at + 8 : at + 16, HID : 2 * HID]
    packed[0 : grads.shape[0], :] = grads[...].astype(BF16)
    packed[grads.shape[0] :, :] = jnp.zeros((packed.shape[0] - grads.shape[0], LANES), BF16)


def last_kernel(da_one, cot, w_first_flip, d_primal, strip, dx):
    rows1 = RY + 2
    first, last = lane_masks((8, LANES))
    for z in range(CZ):
        for y in range(0, RY, 2):
            taps = jnp.dot(w_first_flip[...], window(da_one, rows1, z, y), preferred_element_type=F32)
            for s in range(2):
                at = (z * RY + y + s) * 8
                dx[at : at + 8, :] = shift_sum(taps[:, s * LANES : (s + 1) * LANES], first, last)
    fields = []
    for z in range(CZ):
        for c in range(5):
            d_primal[c, z] = cot[c, z] + dx[pl.ds(z * RY * 8 + c, RY, stride=8), :]
        fields.append(dx[pl.ds(z * RY * 8 + 5, RY, stride=8), :])
    strip[...] = jnp.concatenate(fields, axis=0).astype(BF16)


def dual_kernel(meta, strips, tiles, foots, prints, out, codes):
    view_at = meta[0]
    foot_count = prints.shape[0]
    ranks = strips.shape[0]
    views = tiles.shape[0] // 2 // ranks
    own = pl.ds(pl.multiple_of(view_at * views * 2, views * 2), views * 2)
    codes[...] = (tiles[own, :] * foot_count + foots[own, :]).astype(F32)
    taps = [codes[pl.ds(k, views, stride=2), :] for k in range(2)]
    pieces = [strips[d].astype(F32) for d in range(ranks)]
    field = jnp.concatenate(
        [pieces[d][z * RY : (z + 1) * RY] for z in range(CZ) for d in range(ranks)], axis=0
    ).astype(BF16)
    total = jnp.zeros((DTL * views, LANES), F32)
    contract = (((1,), (1,)), ((), ()))
    for o in range(foot_count):
        counts = jnp.concatenate(
            [
                sum(jnp.where(tap == float(g * foot_count + o), 1.0, 0.0) for tap in taps)
                for g in range(DTL)
            ],
            axis=0,
        ).astype(BF16)
        part = jnp.dot(counts, field, preferred_element_type=F32)
        high = part.astype(BF16)
        low = (part - high.astype(F32)).astype(BF16)
        both = lax.dot_general(
            jnp.concatenate([high, low], axis=0), prints[o], contract, preferred_element_type=F32
        )
        total = total + both[: DTL * views] + both[DTL * views :]
    for g in range(DTL):
        out[pl.ds(g, views, stride=DTL), :] = total[g * views : (g + 1) * views]


def sum_kernel(per, shares, out):
    block = max(per, 8)
    total = shares[...].astype(F32).reshape(shares.shape[0] // block, block, LANES).sum(axis=0)
    step = per
    while step < block:
        total = total + pltpu.roll(total, step, 0)
        step *= 2
    while total.shape[0] < 16:
        total = jnp.concatenate([total, total], axis=0)
    total = total.astype(BF16)
    for at in range(0, out.shape[0], total.shape[0]):
        out[at : at + total.shape[0], :] = total


def sum_call(per):
    def kernel(*refs):
        sum_kernel(per, *refs)

    return kernel


def split_kernel(scale, packed, d_first, d_middle, d_last):
    values = packed[0:432, :].astype(F32) * scale
    for shift in range(3):
        moved = values if shift == 0 else pltpu.roll(values, LANES - shift * HID, 1)
        for a in range(3):
            for b in range(3):
                tap = a * 3 + b
                d_middle[2 - a, 2 - b, 2 - shift] = moved[tap * HID : (tap + 1) * HID, :HID]
                at = 288 + tap * SLOT
                d_first[a, b, shift] = moved[at : at + 6, :HID]
                d_last[2 - a, 2 - b, :, 2 - shift, :] = moved[at + 8 : at + 13, :HID]


def split_call(scale):
    def kernel(*refs):
        split_kernel(scale, *refs)

    return kernel


def flipped(kernel):
    return kernel[::-1, ::-1, ::-1].transpose(0, 1, 2, 4, 3)


def by_taps(kernel, shift):
    o, i = kernel.shape[3], kernel.shape[4]
    kernel = jnp.pad(kernel, ((0, 0),) * 4 + ((shift, SLOT - i - shift),))
    return kernel.transpose(3, 0, 1, 2, 4).reshape(o, 27 * SLOT)


def by_rows(kernel, inputs_to, outputs_to):
    o, i = kernel.shape[3], kernel.shape[4]
    kernel = jnp.pad(
        kernel, ((0, 0), (0, 0), (0, 0), (0, outputs_to - o), (0, inputs_to - i))
    )
    return kernel.transpose(2, 3, 0, 1, 4).reshape(3 * outputs_to, 9 * inputs_to)


def shards(
    primal, dual, footprints, tile_index, footprint_offset, w_first, w_middle, w_last, cotangent
):
    views_here, det_tiles, _ = dual.shape
    all_views, tiles_here, taps = tile_index.shape
    ranks = lax.axis_size("view")
    slabs = lax.axis_size("slab")
    devices = ranks * slabs
    view_at = lax.axis_index("view")
    slab_at = lax.axis_index("slab")
    meta = jnp.stack([view_at]).astype(jnp.int32)
    meta_net = jnp.stack([slab_at, view_at, slabs, ranks]).astype(jnp.int32)
    flat = lambda idx: idx.transpose(0, 2, 1).reshape(all_views * taps, tiles_here)
    tiles, foots = flat(tile_index), flat(footprint_offset)

    packed = pl.pallas_call(
        pack_kernel,
        out_shape=jax.ShapeDtypeStruct((320 + views_here * det_tiles, LANES), BF16),
        in_specs=[pl.BlockSpec(memory_space=pltpu.HBM)] * 3,
        out_specs=vmem_spec(),
        scratch_shapes=[
            pltpu.VMEM((160, LANES), F32),
            pltpu.VMEM((160, LANES), F32),
            pltpu.VMEM((views_here * det_tiles, LANES), BF16),
            pltpu.SemaphoreType.DMA((3,)),
        ],
        compiler_params=PARAMS,
        interpret=INTERPRET,
        name="pack_inputs",
    )(
        in_hbm(primal.reshape(160, LANES)),
        in_hbm(cotangent.reshape(160, LANES)),
        in_hbm(dual.reshape(views_here * det_tiles, LANES)),
    )
    packed = lax.all_gather(packed, "view", axis=0, tiled=False)

    here = pl.pallas_call(
        gather_kernel,
        out_shape=jax.ShapeDtypeStruct((CZ * WY * SENT, LANES), BF16),
        in_specs=[smem_spec()] + [vmem_spec()] * 4,
        out_specs=vmem_spec(),
        scratch_shapes=[
            pltpu.VMEM((all_views * taps, tiles_here), F32),
            pltpu.VMEM((all_views * det_tiles, LANES), F32),
            pltpu.VMEM((tiles_here, LANES), F32),
            pltpu.VMEM((CZ * WY * SENT, LANES), F32),
        ],
        compiler_params=PARAMS,
        interpret=INTERPRET,
        name="box_rows",
    )(meta, packed, tiles, foots, footprints)

    inner = lambda i: i if i == 0 or i == slabs - 1 else ((i - 1) ^ 1) + 1
    crossed = lax.ppermute(here, "slab", [(i, inner(i)) for i in range(slabs)])
    paired = lax.ppermute(here, "slab", [(i, i ^ 1) for i in range(slabs)])

    w_in = jnp.concatenate([by_taps(w_first, 0), by_taps(flipped(w_last), 8)], axis=0)
    w_mid = by_rows(w_middle, HID, HID)
    w_mid_flip = by_rows(flipped(w_middle), HID, HID)
    w_first_flip = by_rows(flipped(w_first), HID, 8)

    rows3, rows2, rows1 = 140, 96, 60
    da_one, grads = pl.pallas_call(
        net_kernel,
        out_shape=(
            jax.ShapeDtypeStruct((rows1, HID, LANES), BF16),
            jax.ShapeDtypeStruct((2 * devices if devices >= 256 else 32 * devices, LANES), BF16),
        ),
        in_specs=[smem_spec()] + [vmem_spec()] * 6,
        out_specs=(vmem_spec(),) * 2,
        scratch_shapes=[
            pltpu.VMEM((432, LANES), F32),
            pltpu.VMEM((LANES, 4 * LANES), F32),
            pltpu.VMEM((288, 3 * HID), F32),
            pltpu.VMEM((7, 3 * HID, 2 * LANES), F32),
            pltpu.VMEM((7, 3 * HID, 2 * LANES), F32),
            pltpu.VMEM((3 * CZ * WY, 3 * SLOT, LANES), BF16),
            pltpu.VMEM((rows3, HID, LANES), F32),
            pltpu.VMEM((rows3, HID, LANES), F32),
            pltpu.VMEM((rows3, HID, LANES), BF16),
            pltpu.VMEM((rows2, HID, LANES), BF16),
            pltpu.VMEM((rows2, HID, LANES), BF16),
        ],
        compiler_params=PARAMS,
        interpret=INTERPRET,
        name="net_box",
    )(meta_net, paired, here, crossed, w_in, w_mid, w_mid_flip)

    both = ("slab", "view")
    per = grads.shape[0] // devices
    shares = lax.all_to_all(grads.reshape(devices, per, LANES), both, 0, 0, tiled=True)

    d_primal, strip = pl.pallas_call(
        last_kernel,
        out_shape=(
            jax.ShapeDtypeStruct(primal.shape, F32),
            jax.ShapeDtypeStruct((CZ * RY, LANES), BF16),
        ),
        in_specs=[vmem_spec()] * 3,
        out_specs=(vmem_spec(),) * 2,
        scratch_shapes=[pltpu.VMEM((CZ * RY * 8, LANES), F32)],
        compiler_params=PARAMS,
        interpret=INTERPRET,
        name="last_layer",
    )(da_one, cotangent, w_first_flip)

    ring = lambda step: [(i, (i + step) % ranks) for i in range(ranks)]
    others = [lax.ppermute(strip, "view", ring(step)) for step in range(1, ranks)]

    summed = pl.pallas_call(
        sum_call(per),
        out_shape=jax.ShapeDtypeStruct(grads.shape, BF16),
        in_specs=[vmem_spec()],
        out_specs=vmem_spec(),
        compiler_params=PARAMS,
        interpret=INTERPRET,
        name="sum_shares",
    )(shares.reshape(grads.shape))
    whole = lax.all_to_all(summed.reshape(shares.shape), both, 0, 0, tiled=True)
    whole = whole.reshape(grads.shape)

    arrived = jnp.stack([strip] + others)
    order = (view_at - jnp.arange(ranks)) % ranks
    strips = jnp.take(arrived, order, axis=0)
    d_dual = pl.pallas_call(
        dual_kernel,
        out_shape=jax.ShapeDtypeStruct((views_here * det_tiles, LANES), F32),
        in_specs=[smem_spec()] + [vmem_spec()] * 4,
        out_specs=vmem_spec(),
        scratch_shapes=[pltpu.VMEM((views_here * taps, tiles_here), F32)],
        compiler_params=PARAMS,
        interpret=INTERPRET,
        name="dual_views",
    )(meta, strips, tiles, foots, footprints)

    full = slabs * CZ * ranks * RY * LANES
    d_first, d_middle, d_last = pl.pallas_call(
        split_call(1.0 / math.sqrt(full)),
        out_shape=(
            jax.ShapeDtypeStruct((3, 3, 3, 6, HID), F32),
            jax.ShapeDtypeStruct((3, 3, 3, HID, HID), F32),
            jax.ShapeDtypeStruct((3, 3, 5, 3, HID), F32),
        ),
        in_specs=[vmem_spec()],
        out_specs=(vmem_spec(),) * 3,
        compiler_params=PARAMS,
        interpret=INTERPRET,
        name="split_grads",
    )(whole)
    return (
        d_primal,
        d_dual.reshape(dual.shape),
        d_first.transpose(0, 1, 2, 4, 3),
        d_middle,
        d_last.transpose(0, 1, 3, 2, 4),
    )


def solution(mesh):
    placed = (
        P(None, "slab", "view", None),
        P("view", "slab", None),
        P(),
        P(None, "slab", None),
        P(None, "slab", None),
        P(),
        P(),
        P(),
        P(None, "slab", "view", None),
    )
    return jax.shard_map(
        shards,
        mesh=mesh,
        in_specs=placed,
        out_specs=(P(None, "slab", "view", None), P("view", "slab", None), P(), P(), P()),
        check_vma=False,
    )
```

```python
import math

import jax
import jax.numpy as jnp
from jax import lax
from jax.experimental import pallas as pl
from jax.experimental.pallas import tpu as pltpu
from jax.sharding import PartitionSpec as P


F32 = jnp.float32
BF16 = jnp.bfloat16
INTERPRET = False
PARAMS = pltpu.CompilerParams(vmem_limit_bytes=48 << 20)

CZ = 4
RY = 8
REACH = 4
WY = RY + 2 * REACH
LANES = 128
HID = 32
SLOT = 16
DTL = 4
SENT = 11


def smem_spec():
    return pl.BlockSpec(memory_space=pltpu.SMEM)


def vmem_spec():
    return pl.BlockSpec(memory_space=pltpu.VMEM)


def in_hbm(array):
    return array if INTERPRET else pltpu.with_memory_space_constraint(array, pltpu.HBM)


def pack_kernel(primal, cotangent, dual, out, primal_in, cotangent_in, dual_in, sems):
    copies = [
        pltpu.make_async_copy(primal, primal_in, sems.at[0]),
        pltpu.make_async_copy(cotangent, cotangent_in, sems.at[1]),
        pltpu.make_async_copy(dual, dual_in, sems.at[2]),
    ]
    for copy in copies:
        copy.start()
    for copy in copies:
        copy.wait()
    out[0:160, :] = primal_in[...].astype(BF16)
    out[160:320, :] = cotangent_in[...].astype(BF16)
    out[320:, :] = dual_in[...]


def gather_kernel(meta, packed, tiles, foots, prints, out, codes, duals, field, rows):
    view_at = meta[0]
    foot_count = prints.shape[0]
    views = tiles.shape[0] // 2
    codes[...] = (tiles[...] * foot_count + foots[...]).astype(F32)
    by_tap = jnp.concatenate(
        [codes[pl.ds(0, views, stride=2), :], codes[pl.ds(1, views, stride=2), :]], axis=0
    )
    by_tile = by_tap.T
    ranks = packed.shape[0]
    local = views // ranks * DTL
    for d in range(ranks):
        duals[d * local : (d + 1) * local, :] = packed[d, 320 : 320 + local, :].astype(F32)
    stack = []
    for g in range(DTL):
        one = duals[pl.ds(g, views, stride=DTL), :].astype(BF16)
        stack += [one, one]
    dual_rows = jnp.concatenate(stack, axis=0)
    back = jnp.zeros((by_tile.shape[0], LANES), F32)
    for o in range(foot_count):
        counts = jnp.concatenate(
            [
                jnp.where(by_tile == float(g * foot_count + o), 1.0, 0.0).astype(BF16)
                for g in range(DTL)
            ],
            axis=1,
        )
        part = jnp.dot(counts, dual_rows, preferred_element_type=F32)
        high = part.astype(BF16)
        low = (part - high.astype(F32)).astype(BF16)
        back = back + jnp.dot(high, prints[o], preferred_element_type=F32)
        back = back + jnp.dot(low, prints[o], preferred_element_type=F32)
    field[...] = back

    before = jnp.maximum(view_at - 1, 0)
    after = jnp.minimum(view_at + 1, ranks - 1)
    has_before = view_at > 0
    has_after = view_at < ranks - 1
    full_y = RY * ranks

    def place(z, slot, mid, low_side, high_side):
        base = z * WY * SENT + slot
        rows[pl.ds(base, REACH, stride=SENT), :] = jnp.where(has_before, low_side[RY - REACH :], 0.0)
        rows[pl.ds(base + REACH * SENT, RY, stride=SENT), :] = mid
        rows[pl.ds(base + (REACH + RY) * SENT, REACH, stride=SENT), :] = jnp.where(
            has_after, high_side[:REACH], 0.0
        )

    for c in range(10):
        slot = c if c < 5 else c + 1
        mid = packed[view_at, c * 32 : c * 32 + 32, :].astype(F32)
        low_side = packed[before, c * 32 : c * 32 + 32, :].astype(F32)
        high_side = packed[after, c * 32 : c * 32 + 32, :].astype(F32)
        for z in range(CZ):
            cut = slice(z * RY, z * RY + RY)
            place(z, slot, mid[cut], low_side[cut], high_side[cut])
    for z in range(CZ):
        at = lambda rank: field[pl.ds(pl.multiple_of(z * full_y + rank * RY, RY), RY), :]
        place(z, 5, at(view_at), at(before), at(after))
    out[...] = rows[...].astype(BF16)


def lane_masks(shape):
    lane = lax.broadcasted_iota(jnp.int32, shape, 1)
    return lane == 0, lane == LANES - 1


def shift_sum(taps, first, last):
    step = taps.shape[0] // 3
    left = jnp.where(first, 0.0, pltpu.roll(taps[:step], 1, 1))
    right = jnp.where(last, 0.0, pltpu.roll(taps[2 * step :], LANES - 1, 1))
    return taps[step : 2 * step] + left + right


def window(get, width, z, y):
    sides = []
    for ahead in range(2):
        sides.append(
            jnp.concatenate(
                [get((z + a) * width + y + ahead + b) for a in range(3) for b in range(3)], axis=0
            )
        )
    return jnp.concatenate(sides, axis=1)


def side_matrix():
    row = lax.broadcasted_iota(jnp.int32, (LANES, 2 * LANES), 0)
    col = lax.broadcasted_iota(jnp.int32, (LANES, 2 * LANES), 1)
    source = jnp.where(col < LANES, col - 1, col - LANES + 1)
    source = jnp.where(source < LANES, source, -1)
    return jnp.where(row == source, 1.0, 0.0).astype(BF16)


def spread_matrix():
    shape = (WY * SLOT, WY * SENT)
    row = lax.broadcasted_iota(jnp.int32, shape, 0)
    col = lax.broadcasted_iota(jnp.int32, shape, 1)
    slot = row & (SLOT - 1)
    channel = jnp.where(slot < 6, slot, jnp.where((slot >= 8) & (slot < 13), slot - 2, -WY * SENT))
    return jnp.where(col == (row >> 4) * SENT + channel, 1.0, 0.0).astype(BF16)


def pipelined(slices, multiply, finish, first_buf, second_buf):
    bufs = (first_buf, second_buf)
    multiply(slices[0], first_buf)
    for at in range(1, len(slices)):
        multiply(slices[at], bufs[at % 2])
        finish(slices[at - 1], bufs[1 - at % 2])
    finish(slices[-1], bufs[1 - len(slices) % 2])


def place_rows(box, to, rows, sides):
    both = jnp.dot(rows, sides, preferred_element_type=F32).astype(BF16)
    to = slice(to, to + WY)
    box[to, 0:SLOT, :] = both[:, :LANES].reshape(WY, SLOT, LANES)
    box[to, SLOT : 2 * SLOT, :] = rows.reshape(WY, SLOT, LANES)
    box[to, 2 * SLOT : 3 * SLOT, :] = both[:, LANES:].reshape(WY, SLOT, LANES)


def sigmoid(value):
    return 0.5 * jnp.tanh(0.5 * value) + 0.5


def inside_of(slab_at, view_at, slabs, ranks):
    def inside(z, y, reach):
        zz, yy = slab_at * CZ - reach + z, view_at * RY - reach + y
        return (zz >= 0) & (zz < slabs * CZ) & (yy >= 0) & (yy < ranks * RY)

    return inside


def times(weights, get, width, rows):
    def multiply(z, buf):
        for y in range(0, rows, 2):
            buf[y // 2, 0 : weights.shape[0], :] = jnp.dot(
                weights[...], window(get, width, z, y), preferred_element_type=F32
            )

    return multiply


def first_layer(inside, base, z_one, slope, dz_two):
    rows3 = RY + 6

    def finish(z, buf):
        for y in range(rows3):
            half = slice((y % 2) * LANES, (y % 2 + 1) * LANES)
            value = buf[y // 2, 0:HID, half]
            sig = sigmoid(value)
            at = (z - base) * rows3 + y
            z_one[at] = jnp.where(inside(z, y, 3), value * sig, 0.0).astype(BF16)
            slope[at] = sig * (1.0 + value * (1.0 - sig))
            dz_two[at] = buf[y // 2, HID : 2 * HID, half]

    return finish


OWN_SLICES = (4, 5)


def own_kernel(meta, here, w_in, box, z_one, slope, dz_two, buf_a, buf_b):
    inside = inside_of(meta[0], meta[1], meta[2], meta[3])
    sides = side_matrix()
    spread = spread_matrix()
    step = WY * SENT
    for z in range(0, CZ, 2):
        pair = [here[at * step : (at + 1) * step] for at in (z, z + 1)]
        spaced = jnp.dot(
            spread, jnp.concatenate(pair, axis=1), preferred_element_type=F32
        ).astype(BF16)
        for at in range(2):
            place_rows(box, (z + at) * WY, spaced[:, at * LANES : (at + 1) * LANES], sides)
    pipelined(
        OWN_SLICES,
        times(w_in, lambda i: box[i - CZ * WY], WY, RY + 6),
        first_layer(inside, OWN_SLICES[0], z_one, slope, dz_two),
        buf_a,
        buf_b,
    )


def net_kernel(
    meta, paired, crossed, own_box, own_z_one, own_slope, own_dz_two, w_in, w_mid, w_mid_flip,
    da_one, packed,
    grads, ends_grad, mid_grad, buf_a, buf_b, box, slope, dz_two, z_one, z_two, da_two,
):
    slab_at, slabs = meta[0], meta[2]
    inside = inside_of(meta[0], meta[1], meta[2], meta[3])
    sides = side_matrix()
    spread = spread_matrix()
    per = CZ * WY
    step = WY * SENT
    odd = slab_at % 2 == 1
    has_prev, has_next = slab_at > 0, slab_at < slabs - 1
    for part in range(2):
        for z in range(0, CZ, 2):
            pair = []
            for at in (z, z + 1):
                cut = slice(at * step, (at + 1) * step)
                near, far = paired[cut], crossed[cut]
                rows = jnp.where(odd, far, near) if part else jnp.where(odd, near, far)
                pair.append(jnp.where(has_next if part else has_prev, rows, jnp.zeros_like(rows)))
            spaced = jnp.dot(
                spread, jnp.concatenate(pair, axis=1), preferred_element_type=F32
            ).astype(BF16)
            for at in range(2):
                to = part * per + (z + at) * WY
                place_rows(box, to, spaced[:, at * LANES : (at + 1) * LANES], sides)
    first, last = lane_masks((HID, LANES))
    depth3, rows3 = CZ + 6, RY + 6
    depth2, rows2 = CZ + 4, RY + 4
    depth1, rows1 = CZ + 2, RY + 2

    def box_row(i):
        if per <= i < 2 * per:
            return own_box[i - per]
        return box[i if i < per else i - per]

    def from_own(ref, own):
        low, high = OWN_SLICES[0] * rows3, (OWN_SLICES[-1] + 1) * rows3
        return lambda i: own[i - low] if low <= i < high else ref[i]

    z_one_row = from_own(z_one, own_z_one)
    slope_row = from_own(slope, own_slope)
    dz_two_row = from_own(dz_two, own_dz_two)

    pipelined(
        [z for z in range(depth3) if z not in OWN_SLICES],
        times(w_in, box_row, WY, rows3),
        first_layer(inside, 0, z_one, slope, dz_two),
        buf_a,
        buf_b,
    )

    def finish_two(z, buf):
        for y in range(rows2):
            half = slice((y % 2) * LANES, (y % 2 + 1) * LANES)
            value = shift_sum(buf[y // 2, 0 : 3 * HID, half], first, last)
            sig = sigmoid(value)
            at = z * rows2 + y
            z_two[at] = (value * sig).astype(BF16)
            grad = dz_two_row((z + 1) * rows3 + y + 1) * (sig * (1.0 + value * (1.0 - sig)))
            da_two[at] = jnp.where(inside(z, y, 2), grad, 0.0).astype(BF16)

    pipelined(
        range(depth2), times(w_mid, z_one_row, rows3, rows2), finish_two, buf_a, buf_b
    )

    def finish_back(z, buf):
        for y in range(rows1):
            half = slice((y % 2) * LANES, (y % 2 + 1) * LANES)
            value = shift_sum(buf[y // 2, 0 : 3 * HID, half], first, last)
            grad = value * slope_row((z + 2) * rows3 + y + 2)
            da_one[z * rows1 + y] = jnp.where(inside(z, y, 1), grad, 0.0).astype(BF16)

    da_two_row = lambda i: da_two[i]
    pipelined(
        range(depth1), times(w_mid_flip, da_two_row, rows2, rows1), finish_back, buf_a, buf_b
    )

    ends_grad[...] = jnp.zeros(ends_grad.shape, F32)
    mid_grad[...] = jnp.zeros(mid_grad.shape, F32)
    contract = (((1,), (1,)), ((), ()))

    for z in range(CZ):
        inner = [z_one_row((z + 3) * rows3 + 3 + y) for y in range(RY)]
        both = jnp.dot(
            jnp.concatenate(inner, axis=0), sides, preferred_element_type=F32
        ).astype(BF16)
        ends = jnp.concatenate(
            [
                jnp.concatenate(
                    [da_one[(z + 1) * rows1 + y + 1], z_two[(z + 2) * rows2 + y + 2]], axis=0
                )
                for y in range(RY)
            ],
            axis=1,
        )
        mids = jnp.concatenate(
            [
                jnp.concatenate(
                    [
                        both[y * HID : (y + 1) * HID, LANES:],
                        inner[y],
                        both[y * HID : (y + 1) * HID, :LANES],
                    ],
                    axis=0,
                )
                for y in range(RY)
            ],
            axis=1,
        )
        low = jnp.concatenate([window(box_row, WY, z + 3, y + 3) for y in range(0, RY, 2)], axis=1)
        mid = jnp.concatenate([window(da_two_row, rows2, z + 1, y + 1) for y in range(0, RY, 2)], axis=1)
        ends_grad[0 : 2 * HID, 0 : 27 * SLOT] += lax.dot_general(
            ends, low, contract, preferred_element_type=F32
        )
        mid_grad[...] += lax.dot_general(mid, mids, contract, preferred_element_type=F32)

    grads[...] = jnp.zeros(grads.shape, F32)
    grads[0:288, 0 : 3 * HID] = mid_grad[...]
    turned = ends_grad[...].T
    for tap in range(9):
        for shift in range(3):
            at = (tap * 3 + shift) * SLOT
            to = 288 + tap * SLOT
            cut = slice(shift * HID, (shift + 1) * HID)
            grads[to : to + 8, cut] = turned[at : at + 8, 0:HID]
            grads[to + 8 : to + 16, cut] = turned[at + 8 : at + 16, HID : 2 * HID]
    packed[0 : grads.shape[0], :] = grads[...].astype(BF16)
    packed[grads.shape[0] :, :] = jnp.zeros((packed.shape[0] - grads.shape[0], LANES), BF16)


def last_kernel(da_one, cot, w_first_flip, d_primal, strip, dx):
    rows1 = RY + 2
    first, last = lane_masks((8, LANES))
    for z in range(CZ):
        for y in range(0, RY, 2):
            taps = jnp.dot(w_first_flip[...], window(lambda i: da_one[i], rows1, z, y), preferred_element_type=F32)
            for s in range(2):
                at = (z * RY + y + s) * 8
                dx[at : at + 8, :] = shift_sum(taps[:, s * LANES : (s + 1) * LANES], first, last)
    fields = []
    for z in range(CZ):
        for c in range(5):
            d_primal[c, z] = cot[c, z] + dx[pl.ds(z * RY * 8 + c, RY, stride=8), :]
        fields.append(dx[pl.ds(z * RY * 8 + 5, RY, stride=8), :])
    strip[...] = jnp.concatenate(fields, axis=0).astype(BF16)


def dual_kernel(meta, strips, tiles, foots, prints, out, codes):
    view_at = meta[0]
    foot_count = prints.shape[0]
    ranks = strips.shape[0]
    views = tiles.shape[0] // 2 // ranks
    own = pl.ds(pl.multiple_of(view_at * views * 2, views * 2), views * 2)
    codes[...] = (tiles[own, :] * foot_count + foots[own, :]).astype(F32)
    taps = [codes[pl.ds(k, views, stride=2), :] for k in range(2)]
    pieces = [strips[d].astype(F32) for d in range(ranks)]
    field = jnp.concatenate(
        [pieces[d][z * RY : (z + 1) * RY] for z in range(CZ) for d in range(ranks)], axis=0
    ).astype(BF16)
    total = jnp.zeros((DTL * views, LANES), F32)
    contract = (((1,), (1,)), ((), ()))
    for o in range(foot_count):
        counts = jnp.concatenate(
            [
                sum(jnp.where(tap == float(g * foot_count + o), 1.0, 0.0) for tap in taps)
                for g in range(DTL)
            ],
            axis=0,
        ).astype(BF16)
        part = jnp.dot(counts, field, preferred_element_type=F32)
        high = part.astype(BF16)
        low = (part - high.astype(F32)).astype(BF16)
        both = lax.dot_general(
            jnp.concatenate([high, low], axis=0), prints[o], contract, preferred_element_type=F32
        )
        total = total + both[: DTL * views] + both[DTL * views :]
    for g in range(DTL):
        out[pl.ds(g, views, stride=DTL), :] = total[g * views : (g + 1) * views]


def sum_kernel(per, shares, out):
    block = max(per, 8)
    total = shares[...].astype(F32).reshape(shares.shape[0] // block, block, LANES).sum(axis=0)
    step = per
    while step < block:
        total = total + pltpu.roll(total, step, 0)
        step *= 2
    while total.shape[0] < 16:
        total = jnp.concatenate([total, total], axis=0)
    total = total.astype(BF16)
    for at in range(0, out.shape[0], total.shape[0]):
        out[at : at + total.shape[0], :] = total


def sum_call(per):
    def kernel(*refs):
        sum_kernel(per, *refs)

    return kernel


def split_kernel(scale, packed, d_first, d_middle, d_last):
    values = packed[0:432, :].astype(F32) * scale
    for shift in range(3):
        moved = values if shift == 0 else pltpu.roll(values, LANES - shift * HID, 1)
        for a in range(3):
            for b in range(3):
                tap = a * 3 + b
                d_middle[2 - a, 2 - b, 2 - shift] = moved[tap * HID : (tap + 1) * HID, :HID]
                at = 288 + tap * SLOT
                d_first[a, b, shift] = moved[at : at + 6, :HID]
                d_last[2 - a, 2 - b, :, 2 - shift, :] = moved[at + 8 : at + 13, :HID]


def split_call(scale):
    def kernel(*refs):
        split_kernel(scale, *refs)

    return kernel


def flipped(kernel):
    return kernel[::-1, ::-1, ::-1].transpose(0, 1, 2, 4, 3)


def by_taps(kernel, shift):
    o, i = kernel.shape[3], kernel.shape[4]
    kernel = jnp.pad(kernel, ((0, 0),) * 4 + ((shift, SLOT - i - shift),))
    return kernel.transpose(3, 0, 1, 2, 4).reshape(o, 27 * SLOT)


def by_rows(kernel, inputs_to, outputs_to):
    o, i = kernel.shape[3], kernel.shape[4]
    kernel = jnp.pad(
        kernel, ((0, 0), (0, 0), (0, 0), (0, outputs_to - o), (0, inputs_to - i))
    )
    return kernel.transpose(2, 3, 0, 1, 4).reshape(3 * outputs_to, 9 * inputs_to)


def shards(
    primal, dual, footprints, tile_index, footprint_offset, w_first, w_middle, w_last, cotangent
):
    views_here, det_tiles, _ = dual.shape
    all_views, tiles_here, taps = tile_index.shape
    ranks = lax.axis_size("view")
    slabs = lax.axis_size("slab")
    devices = ranks * slabs
    view_at = lax.axis_index("view")
    slab_at = lax.axis_index("slab")
    meta = jnp.stack([view_at]).astype(jnp.int32)
    meta_net = jnp.stack([slab_at, view_at, slabs, ranks]).astype(jnp.int32)
    flat = lambda idx: idx.transpose(0, 2, 1).reshape(all_views * taps, tiles_here)
    tiles, foots = flat(tile_index), flat(footprint_offset)

    packed = pl.pallas_call(
        pack_kernel,
        out_shape=jax.ShapeDtypeStruct((320 + views_here * det_tiles, LANES), BF16),
        in_specs=[pl.BlockSpec(memory_space=pltpu.HBM)] * 3,
        out_specs=vmem_spec(),
        scratch_shapes=[
            pltpu.VMEM((160, LANES), F32),
            pltpu.VMEM((160, LANES), F32),
            pltpu.VMEM((views_here * det_tiles, LANES), BF16),
            pltpu.SemaphoreType.DMA((3,)),
        ],
        compiler_params=PARAMS,
        interpret=INTERPRET,
        name="pack_inputs",
    )(
        in_hbm(primal.reshape(160, LANES)),
        in_hbm(cotangent.reshape(160, LANES)),
        in_hbm(dual.reshape(views_here * det_tiles, LANES)),
    )
    packed = lax.all_gather(packed, "view", axis=0, tiled=False)

    here = pl.pallas_call(
        gather_kernel,
        out_shape=jax.ShapeDtypeStruct((CZ * WY * SENT, LANES), BF16),
        in_specs=[smem_spec()] + [vmem_spec()] * 4,
        out_specs=vmem_spec(),
        scratch_shapes=[
            pltpu.VMEM((all_views * taps, tiles_here), F32),
            pltpu.VMEM((all_views * det_tiles, LANES), F32),
            pltpu.VMEM((tiles_here, LANES), F32),
            pltpu.VMEM((CZ * WY * SENT, LANES), F32),
        ],
        compiler_params=PARAMS,
        interpret=INTERPRET,
        name="box_rows",
    )(meta, packed, tiles, foots, footprints)

    inner = lambda i: i if i == 0 or i == slabs - 1 else ((i - 1) ^ 1) + 1
    crossed = lax.ppermute(here, "slab", [(i, inner(i)) for i in range(slabs)])
    paired = lax.ppermute(here, "slab", [(i, i ^ 1) for i in range(slabs)])

    w_in = jnp.concatenate([by_taps(w_first, 0), by_taps(flipped(w_last), 8)], axis=0)
    w_mid = by_rows(w_middle, HID, HID)
    w_mid_flip = by_rows(flipped(w_middle), HID, HID)
    w_first_flip = by_rows(flipped(w_first), HID, 8)

    rows3, rows2, rows1, rows_own = 140, 96, 60, 28
    own = pl.pallas_call(
        own_kernel,
        out_shape=(
            jax.ShapeDtypeStruct((CZ * WY, 3 * SLOT, LANES), BF16),
            jax.ShapeDtypeStruct((rows_own, HID, LANES), BF16),
            jax.ShapeDtypeStruct((rows_own, HID, LANES), F32),
            jax.ShapeDtypeStruct((rows_own, HID, LANES), F32),
        ),
        in_specs=[smem_spec()] + [vmem_spec()] * 2,
        out_specs=(vmem_spec(),) * 4,
        scratch_shapes=[pltpu.VMEM((7, 2 * HID, 2 * LANES), F32)] * 2,
        compiler_params=PARAMS,
        interpret=INTERPRET,
        name="own_slab",
    )(meta_net, here, w_in)
    da_one, grads = pl.pallas_call(
        net_kernel,
        out_shape=(
            jax.ShapeDtypeStruct((rows1, HID, LANES), BF16),
            jax.ShapeDtypeStruct((2 * devices if devices >= 256 else 32 * devices, LANES), BF16),
        ),
        in_specs=[smem_spec()] + [vmem_spec()] * 9,
        out_specs=(vmem_spec(),) * 2,
        scratch_shapes=[
            pltpu.VMEM((432, LANES), F32),
            pltpu.VMEM((LANES, 4 * LANES), F32),
            pltpu.VMEM((288, 3 * HID), F32),
            pltpu.VMEM((7, 3 * HID, 2 * LANES), F32),
            pltpu.VMEM((7, 3 * HID, 2 * LANES), F32),
            pltpu.VMEM((2 * CZ * WY, 3 * SLOT, LANES), BF16),
            pltpu.VMEM((rows3, HID, LANES), F32),
            pltpu.VMEM((rows3, HID, LANES), F32),
            pltpu.VMEM((rows3, HID, LANES), BF16),
            pltpu.VMEM((rows2, HID, LANES), BF16),
            pltpu.VMEM((rows2, HID, LANES), BF16),
        ],
        compiler_params=PARAMS,
        interpret=INTERPRET,
        name="net_box",
    )(meta_net, paired, crossed, *own, w_in, w_mid, w_mid_flip)

    both = ("slab", "view")
    per = grads.shape[0] // devices
    shares = lax.all_to_all(grads.reshape(devices, per, LANES), both, 0, 0, tiled=True)

    d_primal, strip = pl.pallas_call(
        last_kernel,
        out_shape=(
            jax.ShapeDtypeStruct(primal.shape, F32),
            jax.ShapeDtypeStruct((CZ * RY, LANES), BF16),
        ),
        in_specs=[vmem_spec()] * 3,
        out_specs=(vmem_spec(),) * 2,
        scratch_shapes=[pltpu.VMEM((CZ * RY * 8, LANES), F32)],
        compiler_params=PARAMS,
        interpret=INTERPRET,
        name="last_layer",
    )(da_one, cotangent, w_first_flip)

    ring = lambda step: [(i, (i + step) % ranks) for i in range(ranks)]
    others = [lax.ppermute(strip, "view", ring(step)) for step in range(1, ranks)]

    summed = pl.pallas_call(
        sum_call(per),
        out_shape=jax.ShapeDtypeStruct(grads.shape, BF16),
        in_specs=[vmem_spec()],
        out_specs=vmem_spec(),
        compiler_params=PARAMS,
        interpret=INTERPRET,
        name="sum_shares",
    )(shares.reshape(grads.shape))
    whole = lax.all_to_all(summed.reshape(shares.shape), both, 0, 0, tiled=True)
    whole = whole.reshape(grads.shape)

    arrived = jnp.stack([strip] + others)
    order = (view_at - jnp.arange(ranks)) % ranks
    strips = jnp.take(arrived, order, axis=0)
    d_dual = pl.pallas_call(
        dual_kernel,
        out_shape=jax.ShapeDtypeStruct((views_here * det_tiles, LANES), F32),
        in_specs=[smem_spec()] + [vmem_spec()] * 4,
        out_specs=vmem_spec(),
        scratch_shapes=[pltpu.VMEM((views_here * taps, tiles_here), F32)],
        compiler_params=PARAMS,
        interpret=INTERPRET,
        name="dual_views",
    )(meta, strips, tiles, foots, footprints)

    full = slabs * CZ * ranks * RY * LANES
    d_first, d_middle, d_last = pl.pallas_call(
        split_call(1.0 / math.sqrt(full)),
        out_shape=(
            jax.ShapeDtypeStruct((3, 3, 3, 6, HID), F32),
            jax.ShapeDtypeStruct((3, 3, 3, HID, HID), F32),
            jax.ShapeDtypeStruct((3, 3, 5, 3, HID), F32),
        ),
        in_specs=[vmem_spec()],
        out_specs=(vmem_spec(),) * 3,
        compiler_params=PARAMS,
        interpret=INTERPRET,
        name="split_grads",
    )(whole)
    return (
        d_primal,
        d_dual.reshape(dual.shape),
        d_first.transpose(0, 1, 2, 4, 3),
        d_middle,
        d_last.transpose(0, 1, 3, 2, 4),
    )


def solution(mesh):
    placed = (
        P(None, "slab", "view", None),
        P("view", "slab", None),
        P(),
        P(None, "slab", None),
        P(None, "slab", None),
        P(),
        P(),
        P(),
        P(None, "slab", "view", None),
    )
    return jax.shard_map(
        shards,
        mesh=mesh,
        in_specs=placed,
        out_specs=(P(None, "slab", "view", None), P("view", "slab", None), P(), P(), P()),
        check_vma=False,
    )
```

```python
import math

import jax
import jax.numpy as jnp
from jax import lax
from jax.experimental import pallas as pl
from jax.experimental.pallas import tpu as pltpu
from jax.sharding import PartitionSpec as P


F32 = jnp.float32
BF16 = jnp.bfloat16
INTERPRET = False
PARAMS = pltpu.CompilerParams(vmem_limit_bytes=48 << 20)

CZ = 4
RY = 8
REACH = 4
WY = RY + 2 * REACH
LANES = 128
HID = 32
SLOT = 16
DTL = 4
XS, GS = 6, 5
XR, GR = WY * XS, WY * GS
SENT = XR + GR


def smem_spec():
    return pl.BlockSpec(memory_space=pltpu.SMEM)


def vmem_spec():
    return pl.BlockSpec(memory_space=pltpu.VMEM)


def in_hbm(array):
    return array if INTERPRET else pltpu.with_memory_space_constraint(array, pltpu.HBM)


def pack_kernel(primal, cotangent, dual, out, primal_in, cotangent_in, dual_in, sems):
    copies = [
        pltpu.make_async_copy(primal, primal_in, sems.at[0]),
        pltpu.make_async_copy(cotangent, cotangent_in, sems.at[1]),
        pltpu.make_async_copy(dual, dual_in, sems.at[2]),
    ]
    for copy in copies:
        copy.start()
    for copy in copies:
        copy.wait()
    out[0:160, :] = primal_in[...].astype(BF16)
    out[160:320, :] = cotangent_in[...].astype(BF16)
    out[320:, :] = dual_in[...]


def gather_kernel(
    meta, packed, tiles, foots, prints, out, to_pair, to_cross, codes, duals, field, rows_x, rows_g
):
    odd, view_at = meta[0] % 2, meta[1]
    foot_count = prints.shape[0]
    views = tiles.shape[0] // 2
    codes[...] = (tiles[...] * foot_count + foots[...]).astype(F32)
    by_tap = jnp.concatenate(
        [codes[pl.ds(0, views, stride=2), :], codes[pl.ds(1, views, stride=2), :]], axis=0
    )
    by_tile = by_tap.T
    ranks = packed.shape[0]
    local = views // ranks * DTL
    for d in range(ranks):
        duals[d * local : (d + 1) * local, :] = packed[d, 320 : 320 + local, :].astype(F32)
    stack = []
    for g in range(DTL):
        one = duals[pl.ds(g, views, stride=DTL), :].astype(BF16)
        stack += [one, one]
    dual_rows = jnp.concatenate(stack, axis=0)
    back = jnp.zeros((by_tile.shape[0], LANES), F32)
    for o in range(foot_count):
        counts = jnp.concatenate(
            [
                jnp.where(by_tile == float(g * foot_count + o), 1.0, 0.0).astype(BF16)
                for g in range(DTL)
            ],
            axis=1,
        )
        part = jnp.dot(counts, dual_rows, preferred_element_type=F32)
        high = part.astype(BF16)
        low = (part - high.astype(F32)).astype(BF16)
        back = back + jnp.dot(
            jnp.concatenate([high, low], axis=1),
            jnp.concatenate([prints[o], prints[o]], axis=0),
            preferred_element_type=F32,
        )
    field[...] = back

    before = jnp.maximum(view_at - 1, 0)
    after = jnp.minimum(view_at + 1, ranks - 1)
    has_before = view_at > 0
    has_after = view_at < ranks - 1
    full_y = RY * ranks

    def place(z, slot, mid, low_side, high_side):
        rows, count = (rows_x, XS) if slot < XS else (rows_g, GS)
        base = z * WY * count + slot % XS
        rows[pl.ds(base, REACH, stride=count), :] = jnp.where(has_before, low_side[RY - REACH :], 0.0)
        rows[pl.ds(base + REACH * count, RY, stride=count), :] = mid
        rows[pl.ds(base + (REACH + RY) * count, REACH, stride=count), :] = jnp.where(
            has_after, high_side[:REACH], 0.0
        )

    for c in range(10):
        slot = c if c < 5 else c + 1
        mid = packed[view_at, c * 32 : c * 32 + 32, :].astype(F32)
        low_side = packed[before, c * 32 : c * 32 + 32, :].astype(F32)
        high_side = packed[after, c * 32 : c * 32 + 32, :].astype(F32)
        for z in range(CZ):
            cut = slice(z * RY, z * RY + RY)
            place(z, slot, mid[cut], low_side[cut], high_side[cut])
    for z in range(CZ):
        at = lambda rank: field[pl.ds(pl.multiple_of(z * full_y + rank * RY, RY), RY), :]
        place(z, 5, at(view_at), at(before), at(after))
    for z in range(CZ):
        out[z * SENT : z * SENT + XR, :] = rows_x[z * XR : (z + 1) * XR, :].astype(BF16)
        out[z * SENT + XR : (z + 1) * SENT, :] = rows_g[z * GR : (z + 1) * GR, :].astype(BF16)
    for message, start in ((to_pair, 1 - odd), (to_cross, odd)):
        message[0 : CZ * XR, :] = rows_x[...].astype(BF16)
        message[CZ * XR :, :] = rows_g[
            pl.ds(pl.multiple_of(start * GR, GR), (CZ - 1) * GR), :
        ].astype(BF16)


def lane_masks(shape):
    lane = lax.broadcasted_iota(jnp.int32, shape, 1)
    return lane == 0, lane == LANES - 1


def shift_sum(taps, first, last):
    step = taps.shape[0] // 3
    left = jnp.where(first, 0.0, pltpu.roll(taps[:step], 1, 1))
    right = jnp.where(last, 0.0, pltpu.roll(taps[2 * step :], LANES - 1, 1))
    return taps[step : 2 * step] + left + right


def window(get, width, z, y):
    sides = []
    for ahead in range(2):
        sides.append(
            jnp.concatenate(
                [get((z + a) * width + y + ahead + b) for a in range(3) for b in range(3)], axis=0
            )
        )
    return jnp.concatenate(sides, axis=1)


def side_matrix():
    row = lax.broadcasted_iota(jnp.int32, (LANES, 2 * LANES), 0)
    col = lax.broadcasted_iota(jnp.int32, (LANES, 2 * LANES), 1)
    source = jnp.where(col < LANES, col - 1, col - LANES + 1)
    source = jnp.where(source < LANES, source, -1)
    return jnp.where(row == source, 1.0, 0.0).astype(BF16)


def spread_matrix():
    shape = (WY * SLOT, SENT)
    row = lax.broadcasted_iota(jnp.int32, shape, 0)
    col = lax.broadcasted_iota(jnp.int32, shape, 1)
    slot, y = row & (SLOT - 1), row >> 4
    source = jnp.where(
        slot < XS, y * XS + slot, jnp.where((slot >= 8) & (slot < 13), XR + y * GS + slot - 8, -1)
    )
    return jnp.where(col == source, 1.0, 0.0).astype(BF16)


def pipelined(slices, multiply, finish, first_buf, second_buf):
    bufs = (first_buf, second_buf)
    multiply(slices[0], first_buf)
    for at in range(1, len(slices)):
        multiply(slices[at], bufs[at % 2])
        finish(slices[at - 1], bufs[1 - at % 2])
    finish(slices[-1], bufs[1 - len(slices) % 2])


def place_rows(box, to, rows, sides):
    both = jnp.dot(rows, sides, preferred_element_type=F32).astype(BF16)
    to = slice(to, to + WY)
    box[to, 0:SLOT, :] = both[:, :LANES].reshape(WY, SLOT, LANES)
    box[to, SLOT : 2 * SLOT, :] = rows.reshape(WY, SLOT, LANES)
    box[to, 2 * SLOT : 3 * SLOT, :] = both[:, LANES:].reshape(WY, SLOT, LANES)


def sigmoid(value):
    return 0.5 * jnp.tanh(0.5 * value) + 0.5


def inside_of(slab_at, view_at, slabs, ranks):
    def inside(z, y, reach):
        zz, yy = slab_at * CZ - reach + z, view_at * RY - reach + y
        return (zz >= 0) & (zz < slabs * CZ) & (yy >= 0) & (yy < ranks * RY)

    return inside


def times(weights, get, width, rows):
    def multiply(z, buf):
        for y in range(0, rows, 2):
            buf[y // 2, 0 : weights.shape[0], :] = jnp.dot(
                weights[...], window(get, width, z, y), preferred_element_type=F32
            )

    return multiply


def first_layer(inside, base, z_one, slope, dz_two):
    rows3 = RY + 6

    def finish(z, buf):
        for y in range(rows3):
            half = slice((y % 2) * LANES, (y % 2 + 1) * LANES)
            value = buf[y // 2, 0:HID, half]
            sig = sigmoid(value)
            at = (z - base) * rows3 + y
            z_one[at] = jnp.where(inside(z, y, 3), value * sig, 0.0).astype(BF16)
            slope[at] = sig * (1.0 + value * (1.0 - sig))
            dz_two[at] = buf[y // 2, HID : 2 * HID, half]

    return finish


OWN_SLICES = (4, 5)


def own_kernel(meta, here, w_in, box, z_one, slope, dz_two, buf_a, buf_b):
    inside = inside_of(meta[0], meta[1], meta[2], meta[3])
    sides = side_matrix()
    spread = spread_matrix()
    for z in range(0, CZ, 2):
        pair = [here[at * SENT : (at + 1) * SENT] for at in (z, z + 1)]
        spaced = jnp.dot(
            spread, jnp.concatenate(pair, axis=1), preferred_element_type=F32
        ).astype(BF16)
        for at in range(2):
            place_rows(box, (z + at) * WY, spaced[:, at * LANES : (at + 1) * LANES], sides)
    pipelined(
        OWN_SLICES,
        times(w_in, lambda i: box[i - CZ * WY], WY, RY + 6),
        first_layer(inside, OWN_SLICES[0], z_one, slope, dz_two),
        buf_a,
        buf_b,
    )


def net_kernel(
    meta, paired, crossed, own_box, own_z_one, own_slope, own_dz_two, w_in, w_mid, w_mid_flip,
    da_one, packed,
    grads, ends_grad, mid_grad, buf_a, buf_b, box, slope, dz_two, z_one, z_two, da_two,
):
    slab_at, slabs = meta[0], meta[2]
    inside = inside_of(meta[0], meta[1], meta[2], meta[3])
    sides = side_matrix()
    spread = spread_matrix()
    per = CZ * WY
    odd = slab_at % 2 == 1
    has_prev, has_next = slab_at > 0, slab_at < slabs - 1
    for part in range(2):
        for z in range(0, CZ, 2):
            pair = []
            for at in (z, z + 1):
                first_g = 0 if part else 1
                cuts = [slice(at * XR, (at + 1) * XR)]
                if 0 <= at - first_g < CZ - 1:
                    g_at = CZ * XR + (at - first_g) * GR
                    cuts.append(slice(g_at, g_at + GR))
                pieces = []
                for cut in cuts:
                    near, far = paired[cut], crossed[cut]
                    rows = jnp.where(odd, far, near) if part else jnp.where(odd, near, far)
                    has = has_next if part else has_prev
                    pieces.append(jnp.where(has, rows, jnp.zeros_like(rows)))
                if len(cuts) == 1:
                    pieces.append(jnp.zeros((GR, LANES), BF16))
                pair.append(jnp.concatenate(pieces, axis=0))
            spaced = jnp.dot(
                spread, jnp.concatenate(pair, axis=1), preferred_element_type=F32
            ).astype(BF16)
            for at in range(2):
                to = part * per + (z + at) * WY
                place_rows(box, to, spaced[:, at * LANES : (at + 1) * LANES], sides)
    first, last = lane_masks((HID, LANES))
    depth3, rows3 = CZ + 6, RY + 6
    depth2, rows2 = CZ + 4, RY + 4
    depth1, rows1 = CZ + 2, RY + 2

    def box_row(i):
        if per <= i < 2 * per:
            return own_box[i - per]
        return box[i if i < per else i - per]

    def from_own(ref, own):
        low, high = OWN_SLICES[0] * rows3, (OWN_SLICES[-1] + 1) * rows3
        return lambda i: own[i - low] if low <= i < high else ref[i]

    z_one_row = from_own(z_one, own_z_one)
    slope_row = from_own(slope, own_slope)
    dz_two_row = from_own(dz_two, own_dz_two)

    pipelined(
        [z for z in range(depth3) if z not in OWN_SLICES],
        times(w_in, box_row, WY, rows3),
        first_layer(inside, 0, z_one, slope, dz_two),
        buf_a,
        buf_b,
    )

    def finish_two(z, buf):
        for y in range(rows2):
            half = slice((y % 2) * LANES, (y % 2 + 1) * LANES)
            value = shift_sum(buf[y // 2, 0 : 3 * HID, half], first, last)
            sig = sigmoid(value)
            at = z * rows2 + y
            z_two[at] = (value * sig).astype(BF16)
            grad = dz_two_row((z + 1) * rows3 + y + 1) * (sig * (1.0 + value * (1.0 - sig)))
            da_two[at] = jnp.where(inside(z, y, 2), grad, 0.0).astype(BF16)

    pipelined(
        range(depth2), times(w_mid, z_one_row, rows3, rows2), finish_two, buf_a, buf_b
    )

    def finish_back(z, buf):
        for y in range(rows1):
            half = slice((y % 2) * LANES, (y % 2 + 1) * LANES)
            value = shift_sum(buf[y // 2, 0 : 3 * HID, half], first, last)
            grad = value * slope_row((z + 2) * rows3 + y + 2)
            da_one[z * rows1 + y] = jnp.where(inside(z, y, 1), grad, 0.0).astype(BF16)

    da_two_row = lambda i: da_two[i]
    pipelined(
        range(depth1), times(w_mid_flip, da_two_row, rows2, rows1), finish_back, buf_a, buf_b
    )

    ends_grad[...] = jnp.zeros(ends_grad.shape, F32)
    mid_grad[...] = jnp.zeros(mid_grad.shape, F32)
    contract = (((1,), (1,)), ((), ()))

    for z in range(CZ):
        inner = [z_one_row((z + 3) * rows3 + 3 + y) for y in range(RY)]
        both = jnp.dot(
            jnp.concatenate(inner, axis=0), sides, preferred_element_type=F32
        ).astype(BF16)
        ends = jnp.concatenate(
            [
                jnp.concatenate(
                    [da_one[(z + 1) * rows1 + y + 1], z_two[(z + 2) * rows2 + y + 2]], axis=0
                )
                for y in range(RY)
            ],
            axis=1,
        )
        mids = jnp.concatenate(
            [
                jnp.concatenate(
                    [
                        both[y * HID : (y + 1) * HID, LANES:],
                        inner[y],
                        both[y * HID : (y + 1) * HID, :LANES],
                    ],
                    axis=0,
                )
                for y in range(RY)
            ],
            axis=1,
        )
        low = jnp.concatenate([window(box_row, WY, z + 3, y + 3) for y in range(0, RY, 2)], axis=1)
        mid = jnp.concatenate([window(da_two_row, rows2, z + 1, y + 1) for y in range(0, RY, 2)], axis=1)
        ends_grad[0 : 2 * HID, 0 : 27 * SLOT] += lax.dot_general(
            ends, low, contract, preferred_element_type=F32
        )
        mid_grad[...] += lax.dot_general(mid, mids, contract, preferred_element_type=F32)

    grads[...] = jnp.zeros(grads.shape, F32)
    grads[0:288, 0 : 3 * HID] = mid_grad[...]
    turned = ends_grad[...].T
    for tap in range(9):
        for shift in range(3):
            at = (tap * 3 + shift) * SLOT
            to = 288 + tap * SLOT
            cut = slice(shift * HID, (shift + 1) * HID)
            grads[to : to + 8, cut] = turned[at : at + 8, 0:HID]
            grads[to + 8 : to + 16, cut] = turned[at + 8 : at + 16, HID : 2 * HID]
    packed[0 : grads.shape[0], :] = grads[...].astype(BF16)
    packed[grads.shape[0] :, :] = jnp.zeros((packed.shape[0] - grads.shape[0], LANES), BF16)


def last_kernel(da_one, cot, w_first_flip, d_primal, strip, dx):
    rows1 = RY + 2
    first, last = lane_masks((8, LANES))
    for z in range(CZ):
        for y in range(0, RY, 2):
            taps = jnp.dot(w_first_flip[...], window(lambda i: da_one[i], rows1, z, y), preferred_element_type=F32)
            for s in range(2):
                at = (z * RY + y + s) * 8
                dx[at : at + 8, :] = shift_sum(taps[:, s * LANES : (s + 1) * LANES], first, last)
    fields = []
    for z in range(CZ):
        for c in range(5):
            d_primal[c, z] = cot[c, z] + dx[pl.ds(z * RY * 8 + c, RY, stride=8), :]
        fields.append(dx[pl.ds(z * RY * 8 + 5, RY, stride=8), :])
    strip[...] = jnp.concatenate(fields, axis=0).astype(BF16)


def dual_kernel(meta, strips, tiles, foots, prints, out, codes):
    view_at = meta[0]
    foot_count = prints.shape[0]
    ranks = strips.shape[0]
    views = tiles.shape[0] // 2 // ranks
    own = pl.ds(pl.multiple_of(view_at * views * 2, views * 2), views * 2)
    codes[...] = (tiles[own, :] * foot_count + foots[own, :]).astype(F32)
    taps = [codes[pl.ds(k, views, stride=2), :] for k in range(2)]
    pieces = [strips[d].astype(F32) for d in range(ranks)]
    field = jnp.concatenate(
        [pieces[d][z * RY : (z + 1) * RY] for z in range(CZ) for d in range(ranks)], axis=0
    ).astype(BF16)
    total = jnp.zeros((DTL * views, LANES), F32)
    contract = (((1,), (1,)), ((), ()))
    for o in range(foot_count):
        counts = jnp.concatenate(
            [
                sum(jnp.where(tap == float(g * foot_count + o), 1.0, 0.0) for tap in taps)
                for g in range(DTL)
            ],
            axis=0,
        ).astype(BF16)
        part = jnp.dot(counts, field, preferred_element_type=F32)
        high = part.astype(BF16)
        low = (part - high.astype(F32)).astype(BF16)
        both = lax.dot_general(
            jnp.concatenate([high, low], axis=0), prints[o], contract, preferred_element_type=F32
        )
        total = total + both[: DTL * views] + both[DTL * views :]
    for g in range(DTL):
        out[pl.ds(g, views, stride=DTL), :] = total[g * views : (g + 1) * views]


def sum_kernel(per, shares, out):
    block = max(per, 8)
    total = shares[...].astype(F32).reshape(shares.shape[0] // block, block, LANES).sum(axis=0)
    step = per
    while step < block:
        total = total + pltpu.roll(total, step, 0)
        step *= 2
    while total.shape[0] < 16:
        total = jnp.concatenate([total, total], axis=0)
    total = total.astype(BF16)
    for at in range(0, out.shape[0], total.shape[0]):
        out[at : at + total.shape[0], :] = total


def sum_call(per):
    def kernel(*refs):
        sum_kernel(per, *refs)

    return kernel


def split_kernel(scale, packed, d_first, d_middle, d_last):
    values = packed[0:432, :].astype(F32) * scale
    for shift in range(3):
        moved = values if shift == 0 else pltpu.roll(values, LANES - shift * HID, 1)
        for a in range(3):
            for b in range(3):
                tap = a * 3 + b
                d_middle[2 - a, 2 - b, 2 - shift] = moved[tap * HID : (tap + 1) * HID, :HID]
                at = 288 + tap * SLOT
                d_first[a, b, shift] = moved[at : at + 6, :HID]
                d_last[2 - a, 2 - b, :, 2 - shift, :] = moved[at + 8 : at + 13, :HID]


def split_call(scale):
    def kernel(*refs):
        split_kernel(scale, *refs)

    return kernel


def flipped(kernel):
    return kernel[::-1, ::-1, ::-1].transpose(0, 1, 2, 4, 3)


def by_taps(kernel, shift):
    o, i = kernel.shape[3], kernel.shape[4]
    kernel = jnp.pad(kernel, ((0, 0),) * 4 + ((shift, SLOT - i - shift),))
    return kernel.transpose(3, 0, 1, 2, 4).reshape(o, 27 * SLOT)


def by_rows(kernel, inputs_to, outputs_to):
    o, i = kernel.shape[3], kernel.shape[4]
    kernel = jnp.pad(
        kernel, ((0, 0), (0, 0), (0, 0), (0, outputs_to - o), (0, inputs_to - i))
    )
    return kernel.transpose(2, 3, 0, 1, 4).reshape(3 * outputs_to, 9 * inputs_to)


def shards(
    primal, dual, footprints, tile_index, footprint_offset, w_first, w_middle, w_last, cotangent
):
    views_here, det_tiles, _ = dual.shape
    all_views, tiles_here, taps = tile_index.shape
    ranks = lax.axis_size("view")
    slabs = lax.axis_size("slab")
    devices = ranks * slabs
    view_at = lax.axis_index("view")
    slab_at = lax.axis_index("slab")
    meta = jnp.stack([view_at]).astype(jnp.int32)
    meta_net = jnp.stack([slab_at, view_at, slabs, ranks]).astype(jnp.int32)
    flat = lambda idx: idx.transpose(0, 2, 1).reshape(all_views * taps, tiles_here)
    tiles, foots = flat(tile_index), flat(footprint_offset)

    packed = pl.pallas_call(
        pack_kernel,
        out_shape=jax.ShapeDtypeStruct((320 + views_here * det_tiles, LANES), BF16),
        in_specs=[pl.BlockSpec(memory_space=pltpu.HBM)] * 3,
        out_specs=vmem_spec(),
        scratch_shapes=[
            pltpu.VMEM((160, LANES), F32),
            pltpu.VMEM((160, LANES), F32),
            pltpu.VMEM((views_here * det_tiles, LANES), BF16),
            pltpu.SemaphoreType.DMA((3,)),
        ],
        compiler_params=PARAMS,
        interpret=INTERPRET,
        name="pack_inputs",
    )(
        in_hbm(primal.reshape(160, LANES)),
        in_hbm(cotangent.reshape(160, LANES)),
        in_hbm(dual.reshape(views_here * det_tiles, LANES)),
    )
    packed = lax.all_gather(packed, "view", axis=0, tiled=False)

    sent = (CZ * XR + (CZ - 1) * GR, LANES)
    here, to_pair, to_cross = pl.pallas_call(
        gather_kernel,
        out_shape=(
            jax.ShapeDtypeStruct((CZ * SENT, LANES), BF16),
            jax.ShapeDtypeStruct(sent, BF16),
            jax.ShapeDtypeStruct(sent, BF16),
        ),
        in_specs=[smem_spec()] + [vmem_spec()] * 4,
        out_specs=(vmem_spec(),) * 3,
        scratch_shapes=[
            pltpu.VMEM((all_views * taps, tiles_here), F32),
            pltpu.VMEM((all_views * det_tiles, LANES), F32),
            pltpu.VMEM((tiles_here, LANES), F32),
            pltpu.VMEM((CZ * XR, LANES), F32),
            pltpu.VMEM((CZ * GR, LANES), F32),
        ],
        compiler_params=PARAMS,
        interpret=INTERPRET,
        name="box_rows",
    )(meta_net, packed, tiles, foots, footprints)

    inner = lambda i: i if i == 0 or i == slabs - 1 else ((i - 1) ^ 1) + 1
    crossed = lax.ppermute(to_cross, "slab", [(i, inner(i)) for i in range(slabs)])
    paired = lax.ppermute(to_pair, "slab", [(i, i ^ 1) for i in range(slabs)])

    w_in = jnp.concatenate([by_taps(w_first, 0), by_taps(flipped(w_last), 8)], axis=0)
    w_mid = by_rows(w_middle, HID, HID)
    w_mid_flip = by_rows(flipped(w_middle), HID, HID)
    w_first_flip = by_rows(flipped(w_first), HID, 8)

    rows3, rows2, rows1, rows_own = 140, 96, 60, 28
    own = pl.pallas_call(
        own_kernel,
        out_shape=(
            jax.ShapeDtypeStruct((CZ * WY, 3 * SLOT, LANES), BF16),
            jax.ShapeDtypeStruct((rows_own, HID, LANES), BF16),
            jax.ShapeDtypeStruct((rows_own, HID, LANES), F32),
            jax.ShapeDtypeStruct((rows_own, HID, LANES), F32),
        ),
        in_specs=[smem_spec()] + [vmem_spec()] * 2,
        out_specs=(vmem_spec(),) * 4,
        scratch_shapes=[pltpu.VMEM((7, 2 * HID, 2 * LANES), F32)] * 2,
        compiler_params=PARAMS,
        interpret=INTERPRET,
        name="own_slab",
    )(meta_net, here, w_in)
    da_one, grads = pl.pallas_call(
        net_kernel,
        out_shape=(
            jax.ShapeDtypeStruct((rows1, HID, LANES), BF16),
            jax.ShapeDtypeStruct((2 * devices if devices >= 256 else 32 * devices, LANES), BF16),
        ),
        in_specs=[smem_spec()] + [vmem_spec()] * 9,
        out_specs=(vmem_spec(),) * 2,
        scratch_shapes=[
            pltpu.VMEM((432, LANES), F32),
            pltpu.VMEM((LANES, 4 * LANES), F32),
            pltpu.VMEM((288, 3 * HID), F32),
            pltpu.VMEM((7, 3 * HID, 2 * LANES), F32),
            pltpu.VMEM((7, 3 * HID, 2 * LANES), F32),
            pltpu.VMEM((2 * CZ * WY, 3 * SLOT, LANES), BF16),
            pltpu.VMEM((rows3, HID, LANES), F32),
            pltpu.VMEM((rows3, HID, LANES), F32),
            pltpu.VMEM((rows3, HID, LANES), BF16),
            pltpu.VMEM((rows2, HID, LANES), BF16),
            pltpu.VMEM((rows2, HID, LANES), BF16),
        ],
        compiler_params=PARAMS,
        interpret=INTERPRET,
        name="net_box",
    )(meta_net, paired, crossed, *own, w_in, w_mid, w_mid_flip)

    both = ("slab", "view")
    per = grads.shape[0] // devices
    shares = lax.all_to_all(grads.reshape(devices, per, LANES), both, 0, 0, tiled=True)

    d_primal, strip = pl.pallas_call(
        last_kernel,
        out_shape=(
            jax.ShapeDtypeStruct(primal.shape, F32),
            jax.ShapeDtypeStruct((CZ * RY, LANES), BF16),
        ),
        in_specs=[vmem_spec()] * 3,
        out_specs=(vmem_spec(),) * 2,
        scratch_shapes=[pltpu.VMEM((CZ * RY * 8, LANES), F32)],
        compiler_params=PARAMS,
        interpret=INTERPRET,
        name="last_layer",
    )(da_one, cotangent, w_first_flip)

    ring = lambda step: [(i, (i + step) % ranks) for i in range(ranks)]
    others = [lax.ppermute(strip, "view", ring(step)) for step in range(1, ranks)]

    summed = pl.pallas_call(
        sum_call(per),
        out_shape=jax.ShapeDtypeStruct(grads.shape, BF16),
        in_specs=[vmem_spec()],
        out_specs=vmem_spec(),
        compiler_params=PARAMS,
        interpret=INTERPRET,
        name="sum_shares",
    )(shares.reshape(grads.shape))
    whole = lax.all_to_all(summed.reshape(shares.shape), both, 0, 0, tiled=True)
    whole = whole.reshape(grads.shape)

    arrived = jnp.stack([strip] + others)
    order = (view_at - jnp.arange(ranks)) % ranks
    strips = jnp.take(arrived, order, axis=0)
    d_dual = pl.pallas_call(
        dual_kernel,
        out_shape=jax.ShapeDtypeStruct((views_here * det_tiles, LANES), F32),
        in_specs=[smem_spec()] + [vmem_spec()] * 4,
        out_specs=vmem_spec(),
        scratch_shapes=[pltpu.VMEM((views_here * taps, tiles_here), F32)],
        compiler_params=PARAMS,
        interpret=INTERPRET,
        name="dual_views",
    )(meta, strips, tiles, foots, footprints)

    full = slabs * CZ * ranks * RY * LANES
    d_first, d_middle, d_last = pl.pallas_call(
        split_call(1.0 / math.sqrt(full)),
        out_shape=(
            jax.ShapeDtypeStruct((3, 3, 3, 6, HID), F32),
            jax.ShapeDtypeStruct((3, 3, 3, HID, HID), F32),
            jax.ShapeDtypeStruct((3, 3, 5, 3, HID), F32),
        ),
        in_specs=[vmem_spec()],
        out_specs=(vmem_spec(),) * 3,
        compiler_params=PARAMS,
        interpret=INTERPRET,
        name="split_grads",
    )(whole)
    return (
        d_primal,
        d_dual.reshape(dual.shape),
        d_first.transpose(0, 1, 2, 4, 3),
        d_middle,
        d_last.transpose(0, 1, 3, 2, 4),
    )


def solution(mesh):
    placed = (
        P(None, "slab", "view", None),
        P("view", "slab", None),
        P(),
        P(None, "slab", None),
        P(None, "slab", None),
        P(),
        P(),
        P(),
        P(None, "slab", "view", None),
    )
    return jax.shard_map(
        shards,
        mesh=mesh,
        in_specs=placed,
        out_specs=(P(None, "slab", "view", None), P("view", "slab", None), P(), P(), P()),
        check_vma=False,
    )
```
